128 devices in a mesh: sub: 2 (over x_hi), row: 8 (over z, x_lo), col: 8 (over y, core).
Axes of the slice: x: 4 (x_hi: 2, x_lo: 2; x = x_hi * 2 + x_lo), y: 4, z: 4, core: 2. Of those that a mesh axis runs over, the one named last changes fastest.
Arguments:
- pivot_panel: float32 [2, 1024, 1024], P('sub', 'row', 'col'), may hold values from -8 to 100, as said below
- border_panel: float32 [2, 16384, 1024], P('sub', 'row', 'col'), may hold values from -6 to 6
- window: float32 [2, 10240, 16384], P('sub', 'row', 'col'), may hold values from -6 to 6
- assembly_map: int32 [2, 10240], P('sub', 'row'), may hold values from 0 to 10239, as said below
Outputs:
- pivot_factor: float32 [2, 1024, 1024], P('sub', 'row', 'col')
- border_factor: float32 [2, 16384, 1024], P('sub', 'row', 'col')
- parent: float32 [10240, 16384], P(('sub', 'row'), 'col')
The draws below stay inside these ranges and needn't reach their ends.
Inputs may be any that keep to these rules, and one draw needn't show every extreme that they name: `assembly_map`: for each front the map is a permutation of the parent rows; the 1280 rows of one device block send exactly 80 rows to each block of 640 parent rows. `pivot_panel`: each front's block is symmetric, and its diagonal entry exceeds 1.25 times the sum of magnitudes of the other entries of its row.
All inputs are finite; a program needn't handle non-finite values.
Results may differ from the reference program's by a relative error of at most 0.0001.
Values sent between devices are 32-bit elements; how exact they have to be, the bound alone decides.
A program may use at most 192 MiB of HBM per device.

```python
import math
import jax
import jax.numpy as jnp
from jax import lax

P_SIZE = 1024
NC = 16384
WR_DEV = 1280
WR = 10240
PR_DEV = 640
CAP = 80
N_ROW = 8


def draw_pivot_panel(key, part):
    first_key, second_key = jax.random.split(key, 2)
    normal_part = jax.random.normal(first_key, (2, P_SIZE, P_SIZE), jnp.float32) / math.sqrt(2.0 * P_SIZE)
    symmetric = normal_part + jnp.swapaxes(normal_part, 1, 2)
    identity = jnp.eye(P_SIZE, dtype=jnp.float32)
    off_diag = symmetric * (1.0 - identity)
    row_sums = jnp.sum(jnp.abs(off_diag), axis=2)
    factor = jax.random.uniform(second_key, (2, P_SIZE), jnp.float32, 1.25, 3.0)
    return off_diag + identity * (row_sums * factor)[:, :, None]


def draw_assembly_map(key, part):
    blocks_count = WR // WR_DEV
    groups_count = WR // PR_DEV
    position = jnp.arange(WR_DEV)
    target_group = position // CAP
    within = position % CAP
    row_block = jnp.arange(blocks_count)[:, None]
    front_maps = []
    for front_index in range(2):
        front_key = jax.random.fold_in(key, front_index + 7)
        row_key, slot_key = jax.random.split(front_key)
        perm_rows = jax.vmap(lambda subkey: jax.random.permutation(subkey, WR_DEV))(jax.random.split(row_key, blocks_count))
        slot_perm = jax.vmap(lambda subkey: jax.random.permutation(subkey, PR_DEV))(jax.random.split(slot_key, groups_count))
        slot_index = slot_perm[target_group[None, :], row_block * CAP + within[None, :]]
        parent_row = target_group[None, :] * PR_DEV + slot_index
        target = row_block * WR_DEV + perm_rows
        front_map = jnp.zeros((WR,), jnp.int32).at[target.reshape(-1)].set(parent_row.reshape(-1).astype(jnp.int32))
        front_maps.append(front_map)
    return jnp.stack(front_maps)


def block_scale(stream_key, dims, cuts, smallest, largest):
    loudness = 1.0
    for axis_at, blocks in cuts:
        heights = jax.random.uniform(jax.random.fold_in(jax.random.fold_in(stream_key, 6), axis_at), (blocks,), jnp.float32, smallest / len(cuts), largest / len(cuts))
        loudness = loudness * jnp.repeat(jnp.exp(heights), dims[axis_at] // blocks).reshape((-1,) + (1,) * (len(dims) - 1 - axis_at))
    return loudness


def centred(own_key, shape, deviation, limit, cuts=(), kind=jnp.bfloat16):
    gain = block_scale(own_key, shape, cuts, -0.22, 0.18) if cuts else 1.0
    array = jax.random.normal(own_key, shape, jnp.float32) * deviation * gain
    return jnp.minimum(jnp.maximum(array, -limit), limit).astype(kind)


def setup_inputs(seed: int = 0) -> dict:
    splits = jax.random.split(jax.random.key(seed), 5)
    pivot_panel = draw_pivot_panel(jax.random.fold_in(splits[4], 71), 0)
    border_panel = centred(splits[1], (2, NC, P_SIZE), 1.0, 6.0, ((0, 2), (1, 8), (2, 8)), jnp.float32)
    window = centred(splits[2], (2, WR, NC), 1.0, 6.0, ((0, 2), (1, 8), (2, 8)), jnp.float32)
    assembly_map = draw_assembly_map(jax.random.fold_in(splits[4], 71), 0)
    return {"pivot_panel": pivot_panel, "border_panel": border_panel, "window": window, "assembly_map": assembly_map}


def solve_rows(lower_diag, rows):
    return jax.scipy.linalg.solve_triangular(lower_diag, rows.T, lower=True).T

def reference(pivot_panel, border_panel, window, assembly_map):
    lower_first = jnp.linalg.cholesky(pivot_panel[0])
    lower_second = jnp.linalg.cholesky(pivot_panel[1])
    pivot_factor = jnp.stack([lower_first, lower_second])
    border_factor = jnp.stack([solve_rows(lower_first, border_panel[0]), solve_rows(lower_second, border_panel[1])])
    parent = jnp.zeros((WR, NC), jnp.float32)
    for front_index in range(2):
        border_lower = border_factor[front_index]
        rows_factor = border_lower.reshape(N_ROW, NC // N_ROW, P_SIZE)[:, :WR_DEV].reshape(WR, P_SIZE)
        product = jnp.dot(rows_factor.astype(jnp.float32), border_lower.T.astype(jnp.float32), precision=lax.Precision.HIGHEST, preferred_element_type=jnp.float32)
        updated = window[front_index] - product
        parent = parent.at[assembly_map[front_index]].add(updated)
    return (pivot_factor, border_factor, parent)
```

```python
import functools

import jax
import jax.numpy as jnp
from jax import lax
from jax.experimental import pallas as pl
from jax.experimental.pallas import tpu as pltpu
from jax.sharding import PartitionSpec as P

NB = 128
F32 = jnp.float32
BF16 = jnp.bfloat16


def split(x):
    hi = x.astype(BF16)
    return hi, (x - hi.astype(F32)).astype(BF16)


def dot_nn(a, b):
    return lax.dot_general(a, b, (((1,), (0,)), ((), ())), preferred_element_type=F32)


def dot_nt(a, b):
    return lax.dot_general(a, b, (((1,), (1,)), ((), ())), preferred_element_type=F32)


def dot3_nn(a_hi, a_lo, b_hi, b_lo):
    return dot_nn(jnp.concatenate([a_hi, a_lo, a_hi], axis=1), jnp.concatenate([b_hi, b_hi, b_lo], axis=0))


def dot3_nt(a_hi, a_lo, b_hi, b_lo):
    return dot_nt(jnp.concatenate([a_hi, a_lo, a_hi], axis=1), jnp.concatenate([b_hi, b_hi, b_lo], axis=1))


def eliminate(blocks):
    lane = lax.broadcasted_iota(jnp.int32, (8, NB), 1)
    sub = lax.broadcasted_iota(jnp.int32, (8, NB), 0)
    for j in range(NB):
        g, r = divmod(j, 8)
        at_j = lane == j
        for block in blocks:
            row = jnp.broadcast_to(block[g][r : r + 1, :], (8, NB))
            pivot = jnp.broadcast_to(row[:, j : j + 1], (8, NB))
            inv = 1.0 / pivot
            scaled = jnp.where(at_j, inv, row * inv)
            for i in range(g, NB // 8):
                column = jnp.broadcast_to(block[i][:, j : j + 1], (8, NB))
                kept = jnp.where(at_j, 0.0, block[i])
                new = kept - column * scaled
                if i == g:
                    new = jnp.where(sub > r, new, block[i])
                block[i] = new
    return blocks


def factor_kernel(where_ref, pivot_ref, hi_ref, lo_ref, factor_ref, work, panel):
    fronts = work.shape[0]
    size = work.shape[1]
    steps = size // NB
    own, row_at, col_at = where_ref[0], where_ref[1], where_ref[2]
    for f in range(fronts):
        for r in range(steps):
            for c in range(steps):
                work[f, r * NB : (r + 1) * NB, c * NB : (c + 1) * NB] = pivot_ref[(f * steps + r) * steps + c]
    lane = lax.broadcasted_iota(jnp.int32, (NB, NB), 1)
    sub = lax.broadcasted_iota(jnp.int32, (NB, NB), 0)
    factor_ref[...] = jnp.zeros_like(factor_ref)

    def step(j, carry):
        base = pl.multiple_of(j * NB, NB)
        here = pl.ds(base, NB)
        blocks = []
        for f in range(fronts):
            blocks.append([work[f, pl.ds(base + 8 * i, 8), here] for i in range(NB // 8)])
        blocks = eliminate(blocks)
        columns = lax.broadcasted_iota(jnp.int32, (NB, size), 1)
        rows = lax.broadcasted_iota(jnp.int32, (size, NB), 0)
        for f in range(fronts):
            done = jnp.concatenate(blocks[f], axis=0)
            diag = jnp.sum(jnp.where(lane == sub, done, 0.0), axis=1, keepdims=True)
            scale = lax.rsqrt(diag)
            inverse = jnp.where(lane < sub, done, jnp.where(lane == sub, 1.0, 0.0)) * scale
            upper = jnp.where(lane >= sub, done, 0.0) * scale
            inv_hi, inv_lo = split(inverse)
            below_hi, below_lo = split(work[f, :, here])
            left = dot3_nt(below_hi, below_lo, inv_hi, inv_lo)
            left = jnp.where(rows >= base + NB, left, 0.0)
            panel[f] = left
            work[f, here, here] = jnp.zeros((NB, NB), F32)
            right_hi, right_lo = split(work[f, here, :])
            right = dot3_nn(inv_hi, inv_lo, right_hi, right_lo)
            work[f, here, :] = right
            work[f, here, here] = inverse
            full = work[f, here, :]
            lower = jnp.where(columns < base + NB, full, 0.0)
            low_hi, low_lo = split(lower)
            hi_ref[f, here, :] = low_hi
            lo_ref[f, here, :] = low_lo
            full_hi, full_lo = split(full)
            stacked = jnp.concatenate([full_hi, full_hi, full_lo], axis=0)

            @pl.when(jnp.logical_and(j == col_at, own == f))
            def _():
                factor_ref[...] = jnp.where(
                    row_at == j, upper.T, panel[f, pl.ds(pl.multiple_of(row_at * NB, NB), NB), :]
                )

            def trail(i, carry):
                at = pl.ds(pl.multiple_of(i * NB, NB), NB)
                work[f, at, here] = jnp.zeros((NB, NB), F32)
                l_hi, l_lo = split(panel[f, at, :])
                work[f, at, :] -= dot_nn(jnp.concatenate([l_hi, l_lo, l_hi], axis=1), stacked)
                return carry

            lax.fori_loop(j + 1, steps, trail, 0)
        return carry

    lax.fori_loop(0, steps, step, 0)


def factor_fronts(where, pivots, fronts, size):
    return pl.pallas_call(
        factor_kernel,
        in_specs=[pl.BlockSpec(memory_space=pltpu.SMEM), pl.BlockSpec(memory_space=pltpu.VMEM)],
        out_specs=[pl.BlockSpec(memory_space=pltpu.VMEM)] * 3,
        out_shape=[
            jax.ShapeDtypeStruct((fronts, size, size), BF16),
            jax.ShapeDtypeStruct((fronts, size, size), BF16),
            jax.ShapeDtypeStruct((NB, NB), F32),
        ],
        scratch_shapes=[pltpu.VMEM((fronts, size, size), F32), pltpu.VMEM((fronts, size, NB), F32)],
        compiler_params=pltpu.CompilerParams(vmem_limit_bytes=60 << 20),
        name="factor_fronts",
        cost_estimate=pl.CostEstimate(flops=20_000_000_000, bytes_accessed=16 << 20, transcendentals=0),
    )(where, pivots)


def rows_kernel(rows_ref, inv_hi_ref, inv_lo_ref, hi_ref, lo_ref):
    size = inv_hi_ref.shape[1]
    wide = 256
    raw = jnp.concatenate([rows_ref[k] for k in range(rows_ref.shape[0])], axis=1)
    raw_hi, raw_lo = split(raw)
    solved = []
    for n in range(0, size, wide):
        part = slice(0, n + wide)
        at = slice(n, n + wide)
        solved.append(
            dot3_nt(raw_hi[:, part], raw_lo[:, part], inv_hi_ref[0, at, part], inv_lo_ref[0, at, part])
        )
    solved_hi, solved_lo = split(jnp.concatenate(solved, axis=1))
    for n in range(0, size, wide):
        at = slice(n, n + wide)
        out = dot3_nn(solved_hi[:, n:], solved_lo[:, n:], inv_hi_ref[0, n:, at], inv_lo_ref[0, n:, at])
        hi_ref[0, :, at], lo_ref[0, :, at] = split(out)


def solve_both(rows, inv_hi, inv_lo, tile=320):
    steps, total, _ = rows.shape
    fronts, size, _ = inv_hi.shape
    per = total // fronts
    inv_spec = pl.BlockSpec((1, size, size), lambda f, i: (f, 0, 0))
    out_spec = pl.BlockSpec((1, tile, size), lambda f, i: (f, i, 0))
    return pl.pallas_call(
        rows_kernel,
        grid=(fronts, per // tile),
        in_specs=[pl.BlockSpec((steps, tile, NB), lambda f, i: (0, f * (per // tile) + i, 0)), inv_spec, inv_spec],
        out_specs=[out_spec, out_spec],
        out_shape=[jax.ShapeDtypeStruct((fronts, per, size), BF16)] * 2,
        compiler_params=pltpu.CompilerParams(vmem_limit_bytes=60 << 20),
        name="solve_both",
        cost_estimate=pl.CostEstimate(flops=12_000_000_000, bytes_accessed=18 << 20, transcendentals=0),
    )(rows, inv_hi, inv_lo)


def border_kernel(where_ref, raw_ref, hi_ref, lo_ref, out_ref):
    raw_hi, raw_lo = split(jnp.concatenate([raw_ref[k] for k in range(raw_ref.shape[0])], axis=1))
    out_ref[...] = dot3_nt(raw_hi, raw_lo, hi_ref[0], lo_ref[0])


def solve_border(where, columns, inv_hi, inv_lo, tile=512):
    fronts, size, _ = inv_hi.shape
    steps = size // NB
    rows = columns.shape[1]
    inv_spec = pl.BlockSpec((1, NB, size), lambda i, w: (w[0], w[1], 0))
    return pl.pallas_call(
        border_kernel,
        grid_spec=pltpu.PrefetchScalarGridSpec(
            num_scalar_prefetch=1,
            grid=(rows // tile,),
            in_specs=[pl.BlockSpec((steps, tile, NB), lambda i, w: (w[0], i, 0)), inv_spec, inv_spec],
            out_specs=pl.BlockSpec((tile, NB), lambda i, w: (i, 0)),
        ),
        out_shape=jax.ShapeDtypeStruct((rows, NB), F32),
        compiler_params=pltpu.CompilerParams(vmem_limit_bytes=60 << 20),
        name="solve_border",
        cost_estimate=pl.CostEstimate(flops=1_600_000_000, bytes_accessed=10 << 20, transcendentals=0),
    )(where, columns, inv_hi, inv_lo)


def product_kernel(hi_ref, lo_ref, columns_ref, out_ref):
    fronts = hi_ref.shape[0]
    steps = columns_ref.shape[0] // fronts
    total = None
    for f in range(fronts):
        raw = jnp.concatenate([columns_ref[f * steps + k] for k in range(steps)], axis=1)
        c_hi, c_lo = split(raw)
        part = dot3_nt(hi_ref[f], lo_ref[f], c_hi, c_lo)
        total = part if total is None else total + part
    out_ref[...] = total


def product(rows_hi, rows_lo, columns, tile=256):
    fronts, per, size = rows_hi.shape
    blocks, width, _ = columns.shape
    rows_spec = pl.BlockSpec((fronts, per, size), lambda i: (0, 0, 0), pipeline_mode=pl.Buffered(1))
    return pl.pallas_call(
        product_kernel,
        grid=(width // tile,),
        in_specs=[rows_spec, rows_spec, pl.BlockSpec((blocks, tile, NB), lambda i: (0, i, 0))],
        out_specs=pl.BlockSpec((per, tile), lambda i: (0, i)),
        out_shape=jax.ShapeDtypeStruct((per, width), F32),
        compiler_params=pltpu.CompilerParams(vmem_limit_bytes=60 << 20),
        name="product",
        cost_estimate=pl.CostEstimate(flops=16_000_000_000, bytes_accessed=27 << 20, transcendentals=0),
    )(rows_hi, rows_lo, columns)


def assemble_kernel(place_ref, arrived_ref, product_ref, out_ref):
    per = out_ref.shape[0]

    def group(s, carry):
        base = pl.multiple_of(s * 8, 8)
        picked = []
        for r in range(8):
            first = arrived_ref[pl.ds(place_ref[base + r], 1), :]
            second = arrived_ref[pl.ds(place_ref[per + base + r], 1), :]
            picked.append(first + second)
        out_ref[pl.ds(base, 8), :] = jnp.concatenate(picked, axis=0) - product_ref[pl.ds(base, 8), :]
        return carry

    lax.fori_loop(0, per // 8, group, 0)


def assemble(place, arrived, products, tile=256):
    total, width = arrived.shape
    per = products.shape[0]
    return pl.pallas_call(
        assemble_kernel,
        grid_spec=pltpu.PrefetchScalarGridSpec(
            num_scalar_prefetch=1,
            grid=(width // tile,),
            in_specs=[
                pl.BlockSpec((total, tile), lambda i, w: (0, i)),
                pl.BlockSpec((per, tile), lambda i, w: (0, i)),
            ],
            out_specs=pl.BlockSpec((per, tile), lambda i, w: (0, i)),
        ),
        out_shape=jax.ShapeDtypeStruct((per, width), F32),
        compiler_params=pltpu.CompilerParams(vmem_limit_bytes=60 << 20),
        name="assemble",
        cost_estimate=pl.CostEstimate(flops=4_000_000, bytes_accessed=21 << 20, transcendentals=0),
    )(place, arrived, products)


def per_device(pivot_panel, border_panel, window, assembly_map):
    front = lax.axis_index("sub")
    row_index = lax.axis_index("row")
    col_index = lax.axis_index("col")
    fronts, n_row, n_col = lax.axis_size("sub"), lax.axis_size("row"), lax.axis_size("col")
    pivot_local, border_local, window_local = pivot_panel[0], border_panel[0], window[0]
    size = n_row * pivot_local.shape[0]
    rows_kept, width = window_local.shape
    groups = fronts * n_row
    per = rows_kept // fronts
    capacity = rows_kept // groups
    both = ("sub", "row")
    turn = [(r * n_col + c, c * n_row + r) for r in range(n_row) for c in range(n_col)]

    targets, ordering = lax.sort((assembly_map[0], lax.iota(jnp.int32, rows_kept)), num_keys=1)

    def exchange(x):
        return lax.all_to_all(x, both, split_axis=0, concat_axis=0, tiled=True)

    pivots = lax.all_gather(pivot_local, ("sub", "row", "col"), axis=0)
    columns = lax.ppermute(border_local, ("row", "col"), turn)
    columns = lax.all_gather(columns, both, axis=0)
    slots = exchange((targets % per).reshape(groups, capacity)).reshape(-1)
    arrived_rows = exchange(border_local[:rows_kept][ordering].reshape(groups, capacity, NB)).reshape(rows_kept, NB)
    arrived = exchange(window_local[ordering].reshape(groups, capacity, width)).reshape(rows_kept, width)
    owner = lax.iota(jnp.int32, rows_kept) // per
    _, place = lax.sort((slots + owner * per, lax.iota(jnp.int32, rows_kept)), num_keys=1)
    rows = lax.all_gather(arrived_rows[place], "col", axis=0)

    where = jnp.stack([front, row_index, col_index])
    inv_hi, inv_lo, pivot_factor = factor_fronts(where, pivots, fronts, size)
    turned = solve_border(where, columns, inv_hi, inv_lo)
    border_factor = lax.ppermute(turned, ("row", "col"), turn)
    rows_hi, rows_lo = solve_both(rows, inv_hi, inv_lo)
    products = product(rows_hi, rows_lo, columns)
    parent = assemble(place, arrived, products)
    return (pivot_factor[None], border_factor[None], parent)


def solution(mesh):
    in_specs = (
        P("sub", "row", "col"),
        P("sub", "row", "col"),
        P("sub", "row", "col"),
        P("sub", "row"),
    )
    out_specs = (P("sub", "row", "col"), P("sub", "row", "col"), P(("sub", "row"), "col"))
    return jax.shard_map(
        per_device, mesh=mesh, in_specs=in_specs, out_specs=out_specs, check_vma=False
    )
```

```python
import functools

import jax
import jax.numpy as jnp
from jax import lax
from jax.experimental import pallas as pl
from jax.experimental.pallas import tpu as pltpu
from jax.sharding import PartitionSpec as P

NB = 128
F32 = jnp.float32
BF16 = jnp.bfloat16


def split(x):
    hi = x.astype(BF16)
    return hi, (x - hi.astype(F32)).astype(BF16)


def dot_nn(a, b):
    return lax.dot_general(a, b, (((1,), (0,)), ((), ())), preferred_element_type=F32)


def dot_nt(a, b):
    return lax.dot_general(a, b, (((1,), (1,)), ((), ())), preferred_element_type=F32)


def dot3_nn(a_hi, a_lo, b_hi, b_lo):
    return dot_nn(jnp.concatenate([a_hi, a_lo, a_hi], axis=1), jnp.concatenate([b_hi, b_hi, b_lo], axis=0))


def dot3_nt(a_hi, a_lo, b_hi, b_lo):
    return dot_nt(jnp.concatenate([a_hi, a_lo, a_hi], axis=1), jnp.concatenate([b_hi, b_hi, b_lo], axis=1))


def eliminate(blocks):
    lane = lax.broadcasted_iota(jnp.int32, (8, NB), 1)
    sub = lax.broadcasted_iota(jnp.int32, (8, NB), 0)
    shape = (8, NB)
    for g in range(NB // 8):
        first = 8 * g
        for block in blocks:
            rows = [jnp.broadcast_to(block[g][k : k + 1, :], shape) for k in range(8)]
            scalar = {
                (k, n): jnp.broadcast_to(rows[k][:, first + n : first + n + 1], shape)
                for k in range(8)
                for n in range(k, 8)
            }
            inverse, factor = [], {}
            for k in range(8):
                inv = 1.0 / scalar[k, k]
                inverse.append(inv)
                unit = jnp.where(lane == first + k, 1.0, rows[k])
                for n in range(k + 1, 8):
                    m = scalar[k, n] * inv
                    factor[k, n] = m
                    for q in range(n, 8):
                        scalar[n, q] = scalar[n, q] - m * scalar[k, q]
                    rows[n] = jnp.where(lane == first + k, 0.0, rows[n]) - m * unit
            scaled = []
            for k in range(8):
                hat = jnp.where(lane == first + k, 1.0, rows[k])
                if k < 7:
                    hat = jnp.where(jnp.logical_and(lane > first + k, lane < first + 8), 0.0, hat)
                scaled.append(hat * inverse[k])
            for i in range(g + 1, NB // 8):
                column = [jnp.broadcast_to(block[i][:, first + k : first + k + 1], shape) for k in range(8)]
                for k in range(8):
                    for n in range(k + 1, 8):
                        column[n] = column[n] - column[k] * factor[k, n]
                inside = jnp.logical_and(lane >= first, lane < first + 8)
                rest = jnp.where(inside, 0.0, block[i])
                even = column[0] * scaled[0]
                odd = column[1] * scaled[1]
                for k in range(2, 8, 2):
                    even = even + column[k] * scaled[k]
                    odd = odd + column[k + 1] * scaled[k + 1]
                block[i] = rest - (even + odd)
            own = rows[0]
            for k in range(1, 8):
                own = jnp.where(sub == k, rows[k], own)
            block[g] = own
    return blocks


def factor_kernel(where_ref, pivot_ref, hi_ref, lo_ref, factor_ref, work, panel):
    fronts = work.shape[0]
    size = work.shape[1]
    steps = size // NB
    own, row_at, col_at = where_ref[0], where_ref[1], where_ref[2]
    for f in range(fronts):
        for r in range(steps):
            for c in range(steps):
                work[f, r * NB : (r + 1) * NB, c * NB : (c + 1) * NB] = pivot_ref[c, r, f]
    lane = lax.broadcasted_iota(jnp.int32, (NB, NB), 1)
    sub = lax.broadcasted_iota(jnp.int32, (NB, NB), 0)
    factor_ref[...] = jnp.zeros_like(factor_ref)

    def step(j, carry):
        base = pl.multiple_of(j * NB, NB)
        here = pl.ds(base, NB)
        blocks = []
        for f in range(fronts):
            blocks.append([work[f, pl.ds(base + 8 * i, 8), here] for i in range(NB // 8)])
        blocks = eliminate(blocks)
        columns = lax.broadcasted_iota(jnp.int32, (NB, size), 1)
        rows = lax.broadcasted_iota(jnp.int32, (size, NB), 0)
        for f in range(fronts):
            done = jnp.concatenate(blocks[f], axis=0)
            diag = jnp.sum(jnp.where(lane == sub, done, 0.0), axis=1, keepdims=True)
            scale = lax.rsqrt(diag)
            inverse = jnp.where(lane < sub, done, jnp.where(lane == sub, 1.0, 0.0)) * scale
            upper = jnp.where(lane >= sub, done, 0.0) * scale
            inv_hi, inv_lo = split(inverse)
            below_hi, below_lo = split(work[f, :, here])
            left = dot3_nt(below_hi, below_lo, inv_hi, inv_lo)
            left = jnp.where(rows >= base + NB, left, 0.0)
            panel[f] = left
            work[f, here, here] = jnp.zeros((NB, NB), F32)
            right_hi, right_lo = split(work[f, here, :])
            right = dot3_nn(inv_hi, inv_lo, right_hi, right_lo)
            work[f, here, :] = right
            work[f, here, here] = inverse
            full = work[f, here, :]
            lower = jnp.where(columns < base + NB, full, 0.0)
            low_hi, low_lo = split(lower)
            hi_ref[f, here, :] = low_hi
            lo_ref[f, here, :] = low_lo
            full_hi, full_lo = split(full)
            stacked = jnp.concatenate([full_hi, full_hi, full_lo], axis=0)

            @pl.when(jnp.logical_and(j == col_at, own == f))
            def _():
                factor_ref[...] = jnp.where(
                    row_at == j, upper.T, panel[f, pl.ds(pl.multiple_of(row_at * NB, NB), NB), :]
                )

            def trail(i, carry):
                at = pl.ds(pl.multiple_of(i * NB, NB), NB)
                work[f, at, here] = jnp.zeros((NB, NB), F32)
                l_hi, l_lo = split(panel[f, at, :])
                work[f, at, :] -= dot_nn(jnp.concatenate([l_hi, l_lo, l_hi], axis=1), stacked)
                return carry

            lax.fori_loop(j + 1, steps, trail, 0)
        return carry

    lax.fori_loop(0, steps, step, 0)


def factor_fronts(where, pivots, fronts, size):
    return pl.pallas_call(
        factor_kernel,
        in_specs=[pl.BlockSpec(memory_space=pltpu.SMEM), pl.BlockSpec(memory_space=pltpu.VMEM)],
        out_specs=[pl.BlockSpec(memory_space=pltpu.VMEM)] * 3,
        out_shape=[
            jax.ShapeDtypeStruct((fronts, size, size), BF16),
            jax.ShapeDtypeStruct((fronts, size, size), BF16),
            jax.ShapeDtypeStruct((NB, NB), F32),
        ],
        scratch_shapes=[pltpu.VMEM((fronts, size, size), F32), pltpu.VMEM((fronts, size, NB), F32)],
        compiler_params=pltpu.CompilerParams(vmem_limit_bytes=60 << 20),
        name="factor_fronts",
        cost_estimate=pl.CostEstimate(flops=20_000_000_000, bytes_accessed=16 << 20, transcendentals=0),
    )(where, pivots)


def rows_kernel(rows_ref, inv_hi_ref, inv_lo_ref, hi_ref, lo_ref):
    size = inv_hi_ref.shape[1]
    wide = 256
    raw = jnp.concatenate([rows_ref[k] for k in range(rows_ref.shape[0])], axis=1)
    raw_hi, raw_lo = split(raw)
    solved = []
    for n in range(0, size, wide):
        part = slice(0, n + wide)
        at = slice(n, n + wide)
        solved.append(
            dot3_nt(raw_hi[:, part], raw_lo[:, part], inv_hi_ref[0, at, part], inv_lo_ref[0, at, part])
        )
    solved_hi, solved_lo = split(jnp.concatenate(solved, axis=1))
    for n in range(0, size, wide):
        at = slice(n, n + wide)
        out = dot3_nn(solved_hi[:, n:], solved_lo[:, n:], inv_hi_ref[0, n:, at], inv_lo_ref[0, n:, at])
        hi_ref[0, :, at], lo_ref[0, :, at] = split(out)


def solve_both(rows, inv_hi, inv_lo, tile=320):
    steps, total, _ = rows.shape
    fronts, size, _ = inv_hi.shape
    per = total // fronts
    inv_spec = pl.BlockSpec((1, size, size), lambda f, i: (f, 0, 0))
    out_spec = pl.BlockSpec((1, tile, size), lambda f, i: (f, i, 0))
    return pl.pallas_call(
        rows_kernel,
        grid=(fronts, per // tile),
        in_specs=[pl.BlockSpec((steps, tile, NB), lambda f, i: (0, f * (per // tile) + i, 0)), inv_spec, inv_spec],
        out_specs=[out_spec, out_spec],
        out_shape=[jax.ShapeDtypeStruct((fronts, per, size), BF16)] * 2,
        compiler_params=pltpu.CompilerParams(vmem_limit_bytes=60 << 20),
        name="solve_both",
        cost_estimate=pl.CostEstimate(flops=12_000_000_000, bytes_accessed=18 << 20, transcendentals=0),
    )(rows, inv_hi, inv_lo)


def border_kernel(where_ref, raw_ref, hi_ref, lo_ref, out_ref):
    raw_hi, raw_lo = split(jnp.concatenate([raw_ref[k] for k in range(raw_ref.shape[0])], axis=1))
    out_ref[...] = dot3_nt(raw_hi, raw_lo, hi_ref[0], lo_ref[0])


def solve_border(where, columns, inv_hi, inv_lo, tile=512):
    fronts, size, _ = inv_hi.shape
    steps = size // NB
    rows = columns.shape[2]
    inv_spec = pl.BlockSpec((1, NB, size), lambda i, w: (w[0], w[1], 0))
    return pl.pallas_call(
        border_kernel,
        grid_spec=pltpu.PrefetchScalarGridSpec(
            num_scalar_prefetch=1,
            grid=(rows // tile,),
            in_specs=[pl.BlockSpec((steps, None, tile, NB), lambda i, w: (0, w[0], i, 0)), inv_spec, inv_spec],
            out_specs=pl.BlockSpec((tile, NB), lambda i, w: (i, 0)),
        ),
        out_shape=jax.ShapeDtypeStruct((rows, NB), F32),
        compiler_params=pltpu.CompilerParams(vmem_limit_bytes=60 << 20),
        name="solve_border",
        cost_estimate=pl.CostEstimate(flops=1_600_000_000, bytes_accessed=10 << 20, transcendentals=0),
    )(where, columns, inv_hi, inv_lo)


def product_kernel(hi_ref, lo_ref, columns_ref, out_ref):
    fronts = hi_ref.shape[0]
    steps = columns_ref.shape[0]
    total = None
    for f in range(fronts):
        raw = jnp.concatenate([columns_ref[k, f] for k in range(steps)], axis=1)
        c_hi, c_lo = split(raw)
        part = dot3_nt(hi_ref[f], lo_ref[f], c_hi, c_lo)
        total = part if total is None else total + part
    out_ref[...] = total


def product(rows_hi, rows_lo, columns, tile=256):
    fronts, per, size = rows_hi.shape
    blocks, _, width, _ = columns.shape
    rows_spec = pl.BlockSpec((fronts, per, size), lambda i: (0, 0, 0), pipeline_mode=pl.Buffered(1))
    return pl.pallas_call(
        product_kernel,
        grid=(width // tile,),
        in_specs=[rows_spec, rows_spec, pl.BlockSpec((blocks, fronts, tile, NB), lambda i: (0, 0, i, 0))],
        out_specs=pl.BlockSpec((per, tile), lambda i: (0, i)),
        out_shape=jax.ShapeDtypeStruct((per, width), F32),
        compiler_params=pltpu.CompilerParams(vmem_limit_bytes=60 << 20),
        name="product",
        cost_estimate=pl.CostEstimate(flops=16_000_000_000, bytes_accessed=27 << 20, transcendentals=0),
    )(rows_hi, rows_lo, columns)


def assemble_kernel(place_ref, arrived_ref, product_ref, out_ref):
    per = out_ref.shape[0]

    def group(s, carry):
        base = pl.multiple_of(s * 8, 8)
        picked = []
        for r in range(8):
            first = arrived_ref[pl.ds(place_ref[base + r], 1), :]
            second = arrived_ref[pl.ds(place_ref[per + base + r], 1), :]
            picked.append(first + second)
        out_ref[pl.ds(base, 8), :] = jnp.concatenate(picked, axis=0) - product_ref[pl.ds(base, 8), :]
        return carry

    lax.fori_loop(0, per // 8, group, 0)


def assemble(place, arrived, products, tile=256):
    total, width = arrived.shape
    per = products.shape[0]
    return pl.pallas_call(
        assemble_kernel,
        grid_spec=pltpu.PrefetchScalarGridSpec(
            num_scalar_prefetch=1,
            grid=(width // tile,),
            in_specs=[
                pl.BlockSpec((total, tile), lambda i, w: (0, i)),
                pl.BlockSpec((per, tile), lambda i, w: (0, i)),
            ],
            out_specs=pl.BlockSpec((per, tile), lambda i, w: (0, i)),
        ),
        out_shape=jax.ShapeDtypeStruct((per, width), F32),
        compiler_params=pltpu.CompilerParams(vmem_limit_bytes=60 << 20),
        name="assemble",
        cost_estimate=pl.CostEstimate(flops=4_000_000, bytes_accessed=21 << 20, transcendentals=0),
    )(place, arrived, products)


def per_device(pivot_panel, border_panel, window, assembly_map):
    front = lax.axis_index("sub")
    row_index = lax.axis_index("row")
    col_index = lax.axis_index("col")
    fronts, n_row, n_col = lax.axis_size("sub"), lax.axis_size("row"), lax.axis_size("col")
    pivot_local, border_local, window_local = pivot_panel[0], border_panel[0], window[0]
    size = n_row * pivot_local.shape[0]
    rows_kept, width = window_local.shape
    groups = fronts * n_row
    per = rows_kept // fronts
    capacity = rows_kept // groups
    both = ("sub", "row")
    turn = [(r * n_col + c, c * n_row + r) for r in range(n_row) for c in range(n_col)]

    targets, ordering = lax.sort((assembly_map[0], lax.iota(jnp.int32, rows_kept)), num_keys=1)

    def exchange(x):
        return lax.all_to_all(x, both, split_axis=0, concat_axis=0, tiled=True)

    pivots = pivot_local
    for axis in ("sub", "row", "col"):
        pivots = lax.all_gather(pivots, axis, axis=0)
    columns = lax.ppermute(border_local, ("row", "col"), turn)
    columns = lax.all_gather(lax.all_gather(columns, "sub", axis=0), "row", axis=0)
    slots = exchange((targets % per).reshape(groups, capacity)).reshape(-1)
    arrived_rows = exchange(border_local[:rows_kept][ordering].reshape(groups, capacity, NB)).reshape(rows_kept, NB)
    arrived = exchange(window_local[ordering].reshape(groups, capacity, width)).reshape(rows_kept, width)
    owner = lax.iota(jnp.int32, rows_kept) // per
    _, place = lax.sort((slots + owner * per, lax.iota(jnp.int32, rows_kept)), num_keys=1)
    rows = lax.all_gather(arrived_rows[place], "col", axis=0)

    where = jnp.stack([front, row_index, col_index])
    inv_hi, inv_lo, pivot_factor = factor_fronts(where, pivots, fronts, size)
    turned = solve_border(where, columns, inv_hi, inv_lo)
    border_factor = lax.ppermute(turned, ("row", "col"), turn)
    rows_hi, rows_lo = solve_both(rows, inv_hi, inv_lo)
    products = product(rows_hi, rows_lo, columns)
    parent = assemble(place, arrived, products)
    return (pivot_factor[None], border_factor[None], parent)


def solution(mesh):
    in_specs = (
        P("sub", "row", "col"),
        P("sub", "row", "col"),
        P("sub", "row", "col"),
        P("sub", "row"),
    )
    out_specs = (P("sub", "row", "col"), P("sub", "row", "col"), P(("sub", "row"), "col"))
    return jax.shard_map(
        per_device, mesh=mesh, in_specs=in_specs, out_specs=out_specs, check_vma=False
    )
```

```python
import functools

import jax
import jax.numpy as jnp
from jax import lax
from jax.experimental import pallas as pl
from jax.experimental.pallas import tpu as pltpu
from jax.sharding import PartitionSpec as P

NB = 128
F32 = jnp.float32
BF16 = jnp.bfloat16


def split(x):
    hi = x.astype(BF16)
    return hi, (x - hi.astype(F32)).astype(BF16)


def dot_nn(a, b):
    return lax.dot_general(a, b, (((1,), (0,)), ((), ())), preferred_element_type=F32)


def dot_nt(a, b):
    return lax.dot_general(a, b, (((1,), (1,)), ((), ())), preferred_element_type=F32)


def dot3_nn(a_hi, a_lo, b_hi, b_lo):
    return dot_nn(jnp.concatenate([a_hi, a_lo, a_hi], axis=1), jnp.concatenate([b_hi, b_hi, b_lo], axis=0))


def dot3_nt(a_hi, a_lo, b_hi, b_lo):
    return dot_nt(jnp.concatenate([a_hi, a_lo, a_hi], axis=1), jnp.concatenate([b_hi, b_hi, b_lo], axis=1))


def eliminate(blocks):
    lane = lax.broadcasted_iota(jnp.int32, (8, NB), 1)
    sub = lax.broadcasted_iota(jnp.int32, (8, NB), 0)
    shape = (8, NB)
    for g in range(NB // 8):
        first = 8 * g
        for block in blocks:
            rows = [jnp.broadcast_to(block[g][k : k + 1, :], shape) for k in range(8)]
            scalar = {
                (k, n): jnp.broadcast_to(rows[k][:, first + n : first + n + 1], shape)
                for k in range(8)
                for n in range(k, 8)
            }
            inverse, factor = [], {}
            for k in range(8):
                inv = 1.0 / scalar[k, k]
                inverse.append(inv)
                unit = jnp.where(lane == first + k, 1.0, rows[k])
                for n in range(k + 1, 8):
                    m = scalar[k, n] * inv
                    factor[k, n] = m
                    for q in range(n, 8):
                        scalar[n, q] = scalar[n, q] - m * scalar[k, q]
                    rows[n] = jnp.where(lane == first + k, 0.0, rows[n]) - m * unit
            scaled = []
            for k in range(8):
                hat = jnp.where(lane == first + k, 1.0, rows[k])
                if k < 7:
                    hat = jnp.where(jnp.logical_and(lane > first + k, lane < first + 8), 0.0, hat)
                scaled.append(hat * inverse[k])
            for i in range(g + 1, NB // 8):
                column = [jnp.broadcast_to(block[i][:, first + k : first + k + 1], shape) for k in range(8)]
                for k in range(8):
                    for n in range(k + 1, 8):
                        column[n] = column[n] - column[k] * factor[k, n]
                inside = jnp.logical_and(lane >= first, lane < first + 8)
                rest = jnp.where(inside, 0.0, block[i])
                even = column[0] * scaled[0]
                odd = column[1] * scaled[1]
                for k in range(2, 8, 2):
                    even = even + column[k] * scaled[k]
                    odd = odd + column[k + 1] * scaled[k + 1]
                block[i] = rest - (even + odd)
            own = rows[0]
            for k in range(1, 8):
                own = jnp.where(sub == k, rows[k], own)
            block[g] = own
    return blocks


def factor_kernel(where_ref, pivot_ref, hi_ref, lo_ref, factor_ref, work, panel):
    fronts = work.shape[0]
    size = work.shape[1]
    steps = size // NB
    own, row_at, col_at = where_ref[0], where_ref[1], where_ref[2]
    for f in range(fronts):
        for r in range(steps):
            for c in range(steps):
                work[f, r * NB : (r + 1) * NB, c * NB : (c + 1) * NB] = pivot_ref[c % 2, c // 2, r // 2, 2 * f + r % 2]
    lane = lax.broadcasted_iota(jnp.int32, (NB, NB), 1)
    sub = lax.broadcasted_iota(jnp.int32, (NB, NB), 0)
    factor_ref[...] = jnp.zeros_like(factor_ref)

    def step(j, carry):
        base = pl.multiple_of(j * NB, NB)
        here = pl.ds(base, NB)
        blocks = []
        for f in range(fronts):
            blocks.append([work[f, pl.ds(base + 8 * i, 8), here] for i in range(NB // 8)])
        blocks = eliminate(blocks)
        columns = lax.broadcasted_iota(jnp.int32, (NB, size), 1)
        rows = lax.broadcasted_iota(jnp.int32, (size, NB), 0)
        for f in range(fronts):
            done = jnp.concatenate(blocks[f], axis=0)
            diag = jnp.sum(jnp.where(lane == sub, done, 0.0), axis=1, keepdims=True)
            scale = lax.rsqrt(diag)
            inverse = jnp.where(lane < sub, done, jnp.where(lane == sub, 1.0, 0.0)) * scale
            upper = jnp.where(lane >= sub, done, 0.0) * scale
            inv_hi, inv_lo = split(inverse)
            below_hi, below_lo = split(work[f, :, here])
            left = dot3_nt(below_hi, below_lo, inv_hi, inv_lo)
            left = jnp.where(rows >= base + NB, left, 0.0)
            panel[f] = left
            work[f, here, here] = jnp.zeros((NB, NB), F32)
            right_hi, right_lo = split(work[f, here, :])
            right = dot3_nn(inv_hi, inv_lo, right_hi, right_lo)
            work[f, here, :] = right
            work[f, here, here] = inverse
            full = work[f, here, :]
            lower = jnp.where(columns < base + NB, full, 0.0)
            low_hi, low_lo = split(lower)
            hi_ref[f, here, :] = low_hi
            lo_ref[f, here, :] = low_lo
            full_hi, full_lo = split(full)
            stacked = jnp.concatenate([full_hi, full_hi, full_lo], axis=0)

            @pl.when(jnp.logical_and(j == col_at, own == f))
            def _():
                factor_ref[...] = jnp.where(
                    row_at == j, upper.T, panel[f, pl.ds(pl.multiple_of(row_at * NB, NB), NB), :]
                )

            def trail(i, carry):
                at = pl.ds(pl.multiple_of(i * NB, NB), NB)
                work[f, at, here] = jnp.zeros((NB, NB), F32)
                l_hi, l_lo = split(panel[f, at, :])
                work[f, at, :] -= dot_nn(jnp.concatenate([l_hi, l_lo, l_hi], axis=1), stacked)
                return carry

            lax.fori_loop(j + 1, steps, trail, 0)
        return carry

    lax.fori_loop(0, steps, step, 0)


def factor_fronts(where, pivots, fronts, size):
    return pl.pallas_call(
        factor_kernel,
        in_specs=[pl.BlockSpec(memory_space=pltpu.SMEM), pl.BlockSpec(memory_space=pltpu.VMEM)],
        out_specs=[pl.BlockSpec(memory_space=pltpu.VMEM)] * 3,
        out_shape=[
            jax.ShapeDtypeStruct((fronts, size, size), BF16),
            jax.ShapeDtypeStruct((fronts, size, size), BF16),
            jax.ShapeDtypeStruct((NB, NB), F32),
        ],
        scratch_shapes=[pltpu.VMEM((fronts, size, size), F32), pltpu.VMEM((fronts, size, NB), F32)],
        compiler_params=pltpu.CompilerParams(vmem_limit_bytes=60 << 20),
        name="factor_fronts",
        cost_estimate=pl.CostEstimate(flops=20_000_000_000, bytes_accessed=16 << 20, transcendentals=0),
    )(where, pivots)


MESH = pl.DeviceIdType.MESH
RING = 4


def exchange_kernel(
    pivot_ref, border_ref, rows_ref, slots_ref,
    pivots, half_a, half_b, rows_out, slots_out,
    send, recv, local,
):
    s, r, c = lax.axis_index("sub"), lax.axis_index("row"), lax.axis_index("col")
    x, z, y, core = 2 * s + r % 2, r // 2, c // 2, c % 2
    groups = rows_ref.shape[0]
    group = s * (groups // 2) + r

    def device(x, y, z, core):
        return {"sub": x // 2, "row": 2 * z + x % 2, "col": 2 * y + core}

    def along(axis, d):
        if axis == "x":
            return device((x + d) % RING, y, z, core)
        if axis == "y":
            return device(x, (y + d) % RING, z, core)
        return device(x, y, (z + d) % RING, core)

    def plane(o):
        other = (group + o) % groups
        return other, {"sub": other // (groups // 2), "row": other % (groups // 2), "col": c}

    mate = device(x, y, z, 1 - core)
    turned = {"sub": s, "row": c, "col": r}
    count = [0]

    def copy(src, dst, to):
        n = count[0]
        count[0] += 1
        return pltpu.make_async_remote_copy(
            src_ref=src, dst_ref=dst, send_sem=send.at[n], recv_sem=recv.at[n], device_id=to, device_id_type=MESH
        )

    barrier = pltpu.get_barrier_semaphore()
    peers = [along("y", d) for d in (1, 2, 3)] + [mate, turned] + [plane(o)[1] for o in range(1, groups)]
    for peer in peers[:4] + peers[5:]:
        pl.semaphore_signal(barrier, inc=1, device_id=peer, device_id_type=MESH)

    @pl.when(r != c)
    def _():
        pl.semaphore_signal(barrier, inc=1, device_id=turned, device_id_type=MESH)

    pl.semaphore_wait(barrier, len(peers) - 1 + (r != c).astype(jnp.int32))

    tall = half_a.shape[1]
    half = NB // 2
    one, two = pl.ds(0, half), pl.ds(half, half)

    first = [copy(pivot_ref.at[one], pivots.at[core, y, z, x, one], along("z", d)) for d in (1, 2, 3)]
    first += [copy(pivot_ref.at[two], pivots.at[core, y, z, x, two], along("y", d)) for d in (1, 2, 3)]
    for item in first:
        item.start()
    turn_a = copy(border_ref.at[pl.ds(0, tall)], half_a.at[c // 2], turned)
    turn_b = copy(border_ref.at[pl.ds(tall, tall)], half_b.at[2 * s + c % 2], turned)
    keep_a = pltpu.make_async_copy(border_ref.at[pl.ds(0, tall)], half_a.at[z], local.at[3])
    keep_b = pltpu.make_async_copy(border_ref.at[pl.ds(tall, tall)], half_b.at[x], local.at[4])

    @pl.when(r != c)
    def _():
        turn_a.start()
        turn_b.start()

    @pl.when(r == c)
    def _():
        keep_a.start()
        keep_b.start()

    own = [
        pltpu.make_async_copy(pivot_ref, pivots.at[core, y, z, x], local.at[0]),
        pltpu.make_async_copy(rows_ref.at[group], rows_out.at[core, group], local.at[1]),
        pltpu.make_async_copy(slots_ref.at[group], slots_out.at[group], local.at[2]),
    ]
    for item in own:
        item.start()
    spread = []
    for o in range(1, groups):
        other, to = plane(o)
        spread.append(copy(rows_ref.at[other], rows_out.at[core, group], to))
        spread.append(copy(slots_ref.at[other], slots_out.at[group], to))
    for item in spread:
        item.start()

    own[0].wait()
    for item in first:
        item.wait_recv()
    area_one, area_two = pivots.at[core, y, :, x, one], pivots.at[core, :, z, x, two]
    second = [copy(area_one, area_one, along("x", d)) for d in (1, 2, 3)]
    second += [copy(area_two, area_two, along("x", d)) for d in (1, 2, 3)]
    for item in second:
        item.start()

    @pl.when(r != c)
    def _():
        turn_a.wait_recv()
        turn_b.wait_recv()

    @pl.when(r == c)
    def _():
        keep_a.wait()
        keep_b.wait()

    stage = [copy(half_a.at[z], half_a.at[z], along("z", d)) for d in (1, 2, 3)]
    stage += [copy(half_b.at[x], half_b.at[x], along("x", d)) for d in (1, 2, 3)]

    for item in second:
        item.wait_recv()
    area_one, area_two = pivots.at[core, y, :, :, one], pivots.at[core, :, z, :, two]
    third = [copy(area_one, area_one, along("y", d)) for d in (1, 2, 3)]
    third += [copy(area_two, area_two, along("z", d)) for d in (1, 2, 3)]
    swaps = [copy(area_one, area_one, mate), copy(area_two, area_two, mate)]
    for item in third + swaps + stage:
        item.start()

    own[1].wait()
    own[2].wait()
    for item in spread:
        item.wait_recv()
    swap_rows = copy(rows_out.at[core], rows_out.at[core], mate)
    swap_rows.start()
    for d in (1, 2, 3):
        third[d - 1].wait_recv()
        area = pivots.at[core, (y + RING - d) % RING, :, :, one]
        swaps.append(copy(area, area, mate))
        swaps[-1].start()
        third[d + 2].wait_recv()
        area = pivots.at[core, :, (z + RING - d) % RING, :, two]
        swaps.append(copy(area, area, mate))
        swaps[-1].start()
    for item in swaps + stage + [swap_rows]:
        item.wait_recv()
    for item in first + spread + second + third + swaps + stage + [swap_rows]:
        item.wait_send()

    @pl.when(r != c)
    def _():
        turn_a.wait_send()
        turn_b.wait_send()


def exchange_all(pivot, border, rows, slots):
    groups, capacity, _ = rows.shape
    tall = border.shape[0] // 2
    copies = 3 * 6 + 8 + 2 + 6 + 2 * (groups - 1) + 1
    return pl.pallas_call(
        exchange_kernel,
        in_specs=[pl.BlockSpec(memory_space=pltpu.VMEM)] * 4,
        out_specs=[pl.BlockSpec(memory_space=pl.ANY)] * 5,
        out_shape=[
            jax.ShapeDtypeStruct((2, RING, RING, RING, NB, NB), F32),
            jax.ShapeDtypeStruct((RING, tall, NB), F32),
            jax.ShapeDtypeStruct((RING, tall, NB), F32),
            jax.ShapeDtypeStruct((2, groups, capacity, NB), F32),
            jax.ShapeDtypeStruct(slots.shape, jnp.int32),
        ],
        scratch_shapes=[
            pltpu.SemaphoreType.DMA((copies,)),
            pltpu.SemaphoreType.DMA((copies,)),
            pltpu.SemaphoreType.DMA((5,)),
        ],
        compiler_params=pltpu.CompilerParams(
            collective_id=0, has_side_effects=True, vmem_limit_bytes=60 << 20
        ),
        name="exchange_all",
    )(pivot, border, rows, slots)


def rows_kernel(where_ref, *refs):
    pieces, (inv_hi_ref, inv_lo_ref, hi_ref, lo_ref, raw) = refs[:RING], refs[RING:]
    size = inv_hi_ref.shape[2]
    y = where_ref[2] // 2
    wide = 256
    for d in range(RING):
        at = pl.multiple_of(((y + RING - d) % RING) * 2 * NB, 2 * NB)
        raw[:, pl.ds(at, 2 * NB)] = jnp.concatenate([pieces[d][0], pieces[d][1]], axis=1)
    raw_hi, raw_lo = split(raw[...])
    solved = []
    for n in range(0, size, wide):
        part = slice(0, n + wide)
        at = slice(n, n + wide)
        solved.append(
            dot3_nt(raw_hi[:, part], raw_lo[:, part], inv_hi_ref[0, at, part], inv_lo_ref[0, at, part])
        )
    solved_hi, solved_lo = split(jnp.concatenate(solved, axis=1))
    for n in range(0, size, wide):
        at = slice(n, n + wide)
        out = dot3_nn(solved_hi[:, n:], solved_lo[:, n:], inv_hi_ref[0, n:, at], inv_lo_ref[0, n:, at])
        for q in range(2):
            k = n // NB + q
            into = slice((k // 2) * NB, (k // 2 + 1) * NB)
            hi_ref[k % 2, :, into], lo_ref[k % 2, :, into] = split(out[:, q * NB : (q + 1) * NB])


def solve_both(where, pieces, inv_hi, inv_lo, tile=320):
    fronts, size, _ = inv_hi.shape
    per = pieces[0].shape[1] // fronts
    tiles = per // tile
    inv_spec = pl.BlockSpec((1, size, size), lambda f, i, w: (f, 0, 0))
    out_spec = pl.BlockSpec((2, tile, RING * NB), lambda f, i, w: (f, i, 0))
    return pl.pallas_call(
        rows_kernel,
        grid_spec=pltpu.PrefetchScalarGridSpec(
            num_scalar_prefetch=1,
            grid=(fronts, tiles),
            in_specs=[pl.BlockSpec((2, tile, NB), lambda f, i, w: (0, f * tiles + i, 0))] * RING + [inv_spec] * 2,
            out_specs=[out_spec] * 2,
            scratch_shapes=[pltpu.VMEM((tile, size), F32)],
        ),
        out_shape=[jax.ShapeDtypeStruct((2 * fronts, per, RING * NB), BF16)] * 2,
        compiler_params=pltpu.CompilerParams(vmem_limit_bytes=60 << 20),
        name="solve_both",
        cost_estimate=pl.CostEstimate(flops=12_000_000_000, bytes_accessed=18 << 20, transcendentals=0),
    )(where, *pieces, inv_hi, inv_lo)


def product_kernel(where_ref, *refs):
    side_a, side_b = refs[:RING], refs[RING : 2 * RING]
    hi_ref, lo_ref, inv_hi_ref, inv_lo_ref, out_ref, border_ref = refs[2 * RING :]
    front = where_ref[0]
    x, z = 2 * front + where_ref[1] % 2, where_ref[1] // 2

    def lanes(k):
        return pl.ds(pl.multiple_of(k * NB, NB), NB)

    @pl.when(pl.program_id(0) == 0)
    def _():
        out_ref[...] = jnp.zeros_like(out_ref)
        border_ref[...] = jnp.zeros_like(border_ref)
        for d in range(RING):
            at = (x + RING - d) % RING
            c_hi, c_lo = split(jnp.concatenate([side_a[d][k] for k in range(RING)], axis=1))
            out_ref[at // 2] += dot3_nt(hi_ref[at], lo_ref[at], c_hi, c_lo)

            mine = (at // 2 == front).astype(F32).astype(BF16)
            w_hi = jnp.concatenate([inv_hi_ref[0, :, lanes(2 * k + at % 2)] for k in range(RING)], axis=1) * mine
            w_lo = jnp.concatenate([inv_lo_ref[0, :, lanes(2 * k + at % 2)] for k in range(RING)], axis=1) * mine
            border_ref[...] += dot3_nt(c_hi, c_lo, w_hi, w_lo)

    @pl.when(pl.program_id(0) == 1)
    def _():
        border_ref[...] = jnp.zeros_like(border_ref)
        order = [(z + RING - d) % RING for d in range(RING)]
        for f in range(2):
            total = None
            for at in (2 * f, 2 * f + 1):
                c_hi, c_lo = split(jnp.concatenate([side_b[d][at] for d in range(RING)], axis=1))
                t_hi = jnp.concatenate([hi_ref[at, :, lanes(k)] for k in order], axis=1)
                t_lo = jnp.concatenate([lo_ref[at, :, lanes(k)] for k in order], axis=1)
                part = dot3_nt(t_hi, t_lo, c_hi, c_lo)
                total = part if total is None else total + part

                mine = (f == front).astype(F32).astype(BF16)
                w_hi = jnp.concatenate([inv_hi_ref[0, :, lanes(2 * k + at % 2)] for k in order], axis=1) * mine
                w_lo = jnp.concatenate([inv_lo_ref[0, :, lanes(2 * k + at % 2)] for k in order], axis=1) * mine
                border_ref[...] += dot3_nt(c_hi, c_lo, w_hi, w_lo)

            out_ref[f] = total


def product(where, side_a, side_b, rows_hi, rows_lo, inv_hi, inv_lo, tile=256):
    _, per, _ = rows_hi.shape
    fronts, size, _ = inv_hi.shape
    tall = side_a[0].shape[1]
    tiles = tall // tile
    rows_spec = pl.BlockSpec(rows_hi.shape, lambda h, i, w: (0, 0, 0), pipeline_mode=pl.Buffered(1))
    inv_spec = pl.BlockSpec((1, NB, size), lambda h, i, w: (w[0], w[1], 0), pipeline_mode=pl.Buffered(1))
    a_spec = pl.BlockSpec((RING, tile, NB), lambda h, i, w: (0, jnp.where(h == 0, i, tiles - 1), 0))
    b_spec = pl.BlockSpec((RING, tile, NB), lambda h, i, w: (0, jnp.where(h == 1, i, 0), 0))
    return pl.pallas_call(
        product_kernel,
        grid_spec=pltpu.PrefetchScalarGridSpec(
            num_scalar_prefetch=1,
            grid=(2, tiles),
            in_specs=[a_spec] * RING + [b_spec] * RING + [rows_spec] * 2 + [inv_spec] * 2,
            out_specs=[
                pl.BlockSpec((fronts, per, tile), lambda h, i, w: (0, 0, h * tiles + i)),
                pl.BlockSpec((tile, NB), lambda h, i, w: (h * tiles + i, 0)),
            ],
        ),
        out_shape=[
            jax.ShapeDtypeStruct((fronts, per, 2 * tall), F32),
            jax.ShapeDtypeStruct((2 * tall, NB), F32),
        ],
        compiler_params=pltpu.CompilerParams(vmem_limit_bytes=60 << 20),
        name="product",
        cost_estimate=pl.CostEstimate(flops=18_000_000_000, bytes_accessed=32 << 20, transcendentals=0),
    )(where, *side_a, *side_b, rows_hi, rows_lo, inv_hi, inv_lo)


def assemble_kernel(place_ref, arrived_ref, product_ref, out_ref, updated):
    per = out_ref.shape[0]
    for f in range(product_ref.shape[0]):
        at = slice(f * per, (f + 1) * per)
        updated[at] = arrived_ref[at] - product_ref[f]

    def group(s, carry):
        base = pl.multiple_of(s * 8, 8)
        picked = []
        for r in range(8):
            first = updated[pl.ds(place_ref[base + r], 1), :]
            second = updated[pl.ds(place_ref[per + base + r], 1), :]
            picked.append(first + second)
        out_ref[pl.ds(base, 8), :] = jnp.concatenate(picked, axis=0)
        return carry

    lax.fori_loop(0, per // 8, group, 0)


def assemble(place, arrived, products, tile=256):
    total, width = arrived.shape
    fronts, per, _ = products.shape
    return pl.pallas_call(
        assemble_kernel,
        grid_spec=pltpu.PrefetchScalarGridSpec(
            num_scalar_prefetch=1,
            grid=(width // tile,),
            in_specs=[
                pl.BlockSpec((total, tile), lambda i, w: (0, i)),
                pl.BlockSpec((fronts, per, tile), lambda i, w: (0, 0, i)),
            ],
            out_specs=pl.BlockSpec((per, tile), lambda i, w: (0, i)),
            scratch_shapes=[pltpu.VMEM((total, tile), F32)],
        ),
        out_shape=jax.ShapeDtypeStruct((per, width), F32),
        compiler_params=pltpu.CompilerParams(vmem_limit_bytes=60 << 20),
        name="assemble",
        cost_estimate=pl.CostEstimate(flops=4_000_000, bytes_accessed=26 << 20, transcendentals=0),
    )(place, arrived, products)


def per_device(pivot_panel, border_panel, window, assembly_map):
    front = lax.axis_index("sub")
    row_index = lax.axis_index("row")
    col_index = lax.axis_index("col")
    fronts, n_row, n_col = lax.axis_size("sub"), lax.axis_size("row"), lax.axis_size("col")
    pivot_local, border_local, window_local = pivot_panel[0], border_panel[0], window[0]
    size = n_row * pivot_local.shape[0]
    rows_kept, width = window_local.shape
    groups = fronts * n_row
    per = rows_kept // fronts
    capacity = rows_kept // groups
    both = ("sub", "row")
    where = jnp.stack([front, row_index, col_index])

    def shifts(axis, d):
        if axis == "y":
            return [(2 * y + k, 2 * ((y + d) % RING) + k) for y in range(RING) for k in range(2)]
        pairs = []
        for x in range(RING):
            for z in range(RING):
                tx, tz = ((x + d) % RING, z) if axis == "x" else (x, (z + d) % RING)
                pairs.append(((x // 2) * n_row + 2 * z + x % 2, (tx // 2) * n_row + 2 * tz + tx % 2))
        return pairs

    targets, ordering = lax.sort((assembly_map[0], lax.iota(jnp.int32, rows_kept)), num_keys=1)
    sent = window_local[ordering].reshape(groups, capacity, width)
    arrived = lax.all_to_all(sent, both, split_axis=0, concat_axis=0, tiled=True).reshape(rows_kept, width)

    slots = jnp.pad((targets % per).reshape(groups, 1, capacity), ((0, 0), (0, 7), (0, NB - capacity)))
    rows = border_local[:rows_kept][ordering].reshape(groups, capacity, NB)
    pivots, half_a, half_b, rows, slots = exchange_all(pivot_local, border_local, rows, slots)

    side_a = [half_a] + [lax.ppermute(half_a, both, shifts("x", d)) for d in (1, 2, 3)]
    side_b = [half_b] + [lax.ppermute(half_b, both, shifts("z", d)) for d in (1, 2, 3)]
    rows = rows.reshape(2, rows_kept, NB)
    pieces = [rows] + [lax.ppermute(rows, "col", shifts("y", d)) for d in (1, 2, 3)]

    owner = lax.iota(jnp.int32, rows_kept) // per
    _, place = lax.sort(
        (slots[:, 0, :capacity].reshape(-1) + owner * per, lax.iota(jnp.int32, rows_kept)), num_keys=1
    )
    inv_hi, inv_lo, pivot_factor = factor_fronts(where, pivots, fronts, size)
    rows_hi, rows_lo = solve_both(where, pieces, inv_hi, inv_lo)
    products, turned = product(where, side_a, side_b, rows_hi, rows_lo, inv_hi, inv_lo)
    turn = [(r * n_col + c, c * n_row + r) for r in range(n_row) for c in range(n_col)]
    border_factor = lax.ppermute(turned, ("row", "col"), turn)
    parent = assemble(place, arrived, products)
    return (pivot_factor[None], border_factor[None], parent)


def solution(mesh):
    in_specs = (
        P("sub", "row", "col"),
        P("sub", "row", "col"),
        P("sub", "row", "col"),
        P("sub", "row"),
    )
    out_specs = (P("sub", "row", "col"), P("sub", "row", "col"), P(("sub", "row"), "col"))
    return jax.shard_map(
        per_device, mesh=mesh, in_specs=in_specs, out_specs=out_specs, check_vma=False
    )
```

```python
import functools

import jax
import jax.numpy as jnp
from jax import lax
from jax.experimental import pallas as pl
from jax.experimental.pallas import tpu as pltpu
from jax.sharding import PartitionSpec as P

NB = 128
F32 = jnp.float32
BF16 = jnp.bfloat16


def split(x):
    hi = x.astype(BF16)
    return hi, (x - hi.astype(F32)).astype(BF16)


def dot_nn(a, b):
    return lax.dot_general(a, b, (((1,), (0,)), ((), ())), preferred_element_type=F32)


def dot_nt(a, b):
    return lax.dot_general(a, b, (((1,), (1,)), ((), ())), preferred_element_type=F32)


def dot3_nn(a_hi, a_lo, b_hi, b_lo):
    return dot_nn(jnp.concatenate([a_hi, a_lo, a_hi], axis=1), jnp.concatenate([b_hi, b_hi, b_lo], axis=0))


def dot3_nt(a_hi, a_lo, b_hi, b_lo):
    return dot_nt(jnp.concatenate([a_hi, a_lo, a_hi], axis=1), jnp.concatenate([b_hi, b_hi, b_lo], axis=1))


def eliminate(blocks):
    lane = lax.broadcasted_iota(jnp.int32, (8, NB), 1)
    sub = lax.broadcasted_iota(jnp.int32, (8, NB), 0)
    shape = (8, NB)
    for g in range(NB // 8):
        first = 8 * g
        for block in blocks:
            rows = [jnp.broadcast_to(block[g][k : k + 1, :], shape) for k in range(8)]
            scalar = {
                (k, n): jnp.broadcast_to(rows[k][:, first + n : first + n + 1], shape)
                for k in range(8)
                for n in range(k, 8)
            }
            inverse, factor = [], {}
            for k in range(8):
                inv = 1.0 / scalar[k, k]
                inverse.append(inv)
                unit = jnp.where(lane == first + k, 1.0, rows[k])
                for n in range(k + 1, 8):
                    m = scalar[k, n] * inv
                    factor[k, n] = m
                    for q in range(n, 8):
                        scalar[n, q] = scalar[n, q] - m * scalar[k, q]
                    rows[n] = jnp.where(lane == first + k, 0.0, rows[n]) - m * unit
            scaled = []
            for k in range(8):
                hat = jnp.where(lane == first + k, 1.0, rows[k])
                if k < 7:
                    hat = jnp.where(jnp.logical_and(lane > first + k, lane < first + 8), 0.0, hat)
                scaled.append(hat * inverse[k])
            for i in range(g + 1, NB // 8):
                column = [jnp.broadcast_to(block[i][:, first + k : first + k + 1], shape) for k in range(8)]
                for k in range(8):
                    for n in range(k + 1, 8):
                        column[n] = column[n] - column[k] * factor[k, n]
                inside = jnp.logical_and(lane >= first, lane < first + 8)
                rest = jnp.where(inside, 0.0, block[i])
                even = column[0] * scaled[0]
                odd = column[1] * scaled[1]
                for k in range(2, 8, 2):
                    even = even + column[k] * scaled[k]
                    odd = odd + column[k + 1] * scaled[k + 1]
                block[i] = rest - (even + odd)
            own = rows[0]
            for k in range(1, 8):
                own = jnp.where(sub == k, rows[k], own)
            block[g] = own
    return blocks


def factor_kernel(where_ref, pivot_ref, hi_ref, lo_ref, factor_ref, work, panel):
    fronts = work.shape[0]
    size = work.shape[1]
    steps = size // NB
    row_at, col_at = where_ref[1], where_ref[2]
    for f in range(fronts):
        for r in range(steps):
            for c in range(steps):
                work[f, r * NB : (r + 1) * NB, c * NB : (c + 1) * NB] = pivot_ref[c % 2, c // 2, r // 2, r % 2]
    lane = lax.broadcasted_iota(jnp.int32, (NB, NB), 1)
    sub = lax.broadcasted_iota(jnp.int32, (NB, NB), 0)
    factor_ref[...] = jnp.zeros_like(factor_ref)

    def step(j, carry):
        base = pl.multiple_of(j * NB, NB)
        here = pl.ds(base, NB)
        blocks = []
        for f in range(fronts):
            blocks.append([work[f, pl.ds(base + 8 * i, 8), here] for i in range(NB // 8)])
        blocks = eliminate(blocks)
        columns = lax.broadcasted_iota(jnp.int32, (NB, size), 1)
        rows = lax.broadcasted_iota(jnp.int32, (size, NB), 0)
        for f in range(fronts):
            done = jnp.concatenate(blocks[f], axis=0)
            diag = jnp.sum(jnp.where(lane == sub, done, 0.0), axis=1, keepdims=True)
            scale = lax.rsqrt(diag)
            inverse = jnp.where(lane < sub, done, jnp.where(lane == sub, 1.0, 0.0)) * scale
            upper = jnp.where(lane >= sub, done, 0.0) * scale
            inv_hi, inv_lo = split(inverse)
            below_hi, below_lo = split(work[f, :, here])
            left = dot3_nt(below_hi, below_lo, inv_hi, inv_lo)
            left = jnp.where(rows >= base + NB, left, 0.0)
            panel[f] = left
            work[f, here, here] = jnp.zeros((NB, NB), F32)
            right_hi, right_lo = split(work[f, here, :])
            right = dot3_nn(inv_hi, inv_lo, right_hi, right_lo)
            work[f, here, :] = right
            work[f, here, here] = inverse
            full = work[f, here, :]
            lower = jnp.where(columns < base + NB, full, 0.0)
            low_hi, low_lo = split(lower)
            hi_ref[f, here, :] = low_hi
            lo_ref[f, here, :] = low_lo
            full_hi, full_lo = split(full)
            stacked = jnp.concatenate([full_hi, full_hi, full_lo], axis=0)

            @pl.when(j == col_at)
            def _():
                factor_ref[...] = jnp.where(
                    row_at == j, upper.T, panel[f, pl.ds(pl.multiple_of(row_at * NB, NB), NB), :]
                )

            def trail(i, carry):
                at = pl.ds(pl.multiple_of(i * NB, NB), NB)
                work[f, at, here] = jnp.zeros((NB, NB), F32)
                l_hi, l_lo = split(panel[f, at, :])
                work[f, at, :] -= dot_nn(jnp.concatenate([l_hi, l_lo, l_hi], axis=1), stacked)
                return carry

            lax.fori_loop(j + 1, steps, trail, 0)
        return carry

    lax.fori_loop(0, steps, step, 0)


def factor_fronts(where, pivots, fronts, size):
    return pl.pallas_call(
        factor_kernel,
        in_specs=[pl.BlockSpec(memory_space=pltpu.SMEM), pl.BlockSpec(memory_space=pltpu.VMEM)],
        out_specs=[pl.BlockSpec(memory_space=pltpu.VMEM)] * 3,
        out_shape=[
            jax.ShapeDtypeStruct((fronts, size, size), BF16),
            jax.ShapeDtypeStruct((fronts, size, size), BF16),
            jax.ShapeDtypeStruct((NB, NB), F32),
        ],
        scratch_shapes=[pltpu.VMEM((fronts, size, size), F32), pltpu.VMEM((fronts, size, NB), F32)],
        compiler_params=pltpu.CompilerParams(vmem_limit_bytes=60 << 20),
        name="factor_fronts",
        cost_estimate=pl.CostEstimate(flops=20_000_000_000, bytes_accessed=16 << 20, transcendentals=0),
    )(where, pivots)


MESH = pl.DeviceIdType.MESH
RING = 4


def exchange_kernel(pivot_ref, border_ref, pivots, half_a, half_b, rows_out, send, recv, local):
    s, r, c = lax.axis_index("sub"), lax.axis_index("row"), lax.axis_index("col")
    low, z, y, core = r % 2, r // 2, c // 2, c % 2

    def device(low, y, z, core):
        return {"sub": s, "row": 2 * z + low, "col": 2 * y + core}

    along_y = [device(low, (y + d) % RING, z, core) for d in (1, 2, 3)]
    along_z = [device(low, y, (z + d) % RING, core) for d in (1, 2, 3)]
    beside = device(1 - low, y, z, core)
    mate = device(low, y, z, 1 - core)
    turned = {"sub": s, "row": c, "col": r}
    count = [0]

    def copy(src, dst, to):
        n = count[0]
        count[0] += 1
        return pltpu.make_async_remote_copy(
            src_ref=src, dst_ref=dst, send_sem=send.at[n], recv_sem=recv.at[n], device_id=to, device_id_type=MESH
        )

    barrier = pltpu.get_barrier_semaphore()
    peers = along_y + along_z + [beside, mate]
    for peer in peers:
        pl.semaphore_signal(barrier, inc=1, device_id=peer, device_id_type=MESH)

    @pl.when(r != c)
    def _():
        pl.semaphore_signal(barrier, inc=1, device_id=turned, device_id_type=MESH)

    pl.semaphore_wait(barrier, len(peers) + (r != c).astype(jnp.int32))

    tall = half_a.shape[1]
    kept = rows_out.shape[1]
    half = NB // 2
    one, two = pl.ds(0, half), pl.ds(half, half)

    first = [copy(pivot_ref.at[one], pivots.at[core, y, z, low, one], to) for to in along_z]
    first += [copy(pivot_ref.at[two], pivots.at[core, y, z, low, two], to) for to in along_y]
    for item in first:
        item.start()
    own = [
        pltpu.make_async_copy(pivot_ref, pivots.at[core, y, z, low], local.at[0]),
        pltpu.make_async_copy(border_ref.at[pl.ds(0, kept)], rows_out.at[core], local.at[1]),
    ]
    for item in own:
        item.start()
    swap_rows = copy(border_ref.at[pl.ds(0, kept)], rows_out.at[core], mate)
    swap_rows.start()
    turn_a = copy(border_ref.at[pl.ds(0, tall)], half_a.at[c // 2], turned)
    turn_b = copy(border_ref.at[pl.ds(tall, tall)], half_b.at[c % 2], turned)
    keep_a = pltpu.make_async_copy(border_ref.at[pl.ds(0, tall)], half_a.at[z], local.at[2])
    keep_b = pltpu.make_async_copy(border_ref.at[pl.ds(tall, tall)], half_b.at[low], local.at[3])

    own[0].wait()
    for item in first:
        item.wait_recv()
    area_one, area_two = pivots.at[core, y, :, low, one], pivots.at[core, :, z, low, two]
    second = [copy(area_one, area_one, beside), copy(area_two, area_two, beside)]
    for item in second:
        item.start()

    for item in second:
        item.wait_recv()
    area_one, area_two = pivots.at[core, y, :, :, one], pivots.at[core, :, z, :, two]
    third = [copy(area_one, area_one, to) for to in along_y]
    third += [copy(area_two, area_two, to) for to in along_z]
    swaps = [copy(area_one, area_one, mate), copy(area_two, area_two, mate)]
    for item in third + swaps:
        item.start()

    @pl.when(r != c)
    def _():
        turn_a.start()
        turn_b.start()

    @pl.when(r == c)
    def _():
        keep_a.start()
        keep_b.start()

    for d in (1, 2, 3):
        third[d - 1].wait_recv()
        area = pivots.at[core, (y + RING - d) % RING, :, :, one]
        swaps.append(copy(area, area, mate))
        swaps[-1].start()
        third[d + 2].wait_recv()
        area = pivots.at[core, :, (z + RING - d) % RING, :, two]
        swaps.append(copy(area, area, mate))
        swaps[-1].start()

    @pl.when(r != c)
    def _():
        turn_a.wait_recv()
        turn_b.wait_recv()

    @pl.when(r == c)
    def _():
        keep_a.wait()
        keep_b.wait()

    stage = [copy(half_a.at[z], half_a.at[z], to) for to in along_z]
    stage += [copy(half_b.at[low], half_b.at[low], beside)]
    for item in stage:
        item.start()
    own[1].wait()
    for item in swaps + stage + [swap_rows]:
        item.wait_recv()
    for item in first + second + third + swaps + stage + [swap_rows]:
        item.wait_send()

    @pl.when(r != c)
    def _():
        turn_a.wait_send()
        turn_b.wait_send()


def exchange_all(pivot, border, kept):
    tall = border.shape[0] // 2
    copies = 32
    return pl.pallas_call(
        exchange_kernel,
        in_specs=[pl.BlockSpec(memory_space=pltpu.VMEM)] * 2,
        out_specs=[pl.BlockSpec(memory_space=pl.ANY)] * 4,
        out_shape=[
            jax.ShapeDtypeStruct((2, RING, RING, 2, NB, NB), F32),
            jax.ShapeDtypeStruct((RING, tall, NB), F32),
            jax.ShapeDtypeStruct((2, tall, NB), F32),
            jax.ShapeDtypeStruct((2, kept, NB), F32),
        ],
        scratch_shapes=[
            pltpu.SemaphoreType.DMA((copies,)),
            pltpu.SemaphoreType.DMA((copies,)),
            pltpu.SemaphoreType.DMA((4,)),
        ],
        compiler_params=pltpu.CompilerParams(
            collective_id=0, has_side_effects=True, vmem_limit_bytes=60 << 20
        ),
        name="exchange_all",
    )(pivot, border)


def rows_kernel(where_ref, *refs):
    pieces, (inv_hi_ref, inv_lo_ref, hi_ref, lo_ref, raw) = refs[:RING], refs[RING:]
    size = inv_hi_ref.shape[2]
    y = where_ref[2] // 2
    wide = 256
    for d in range(RING):
        at = pl.multiple_of(((y + RING - d) % RING) * 2 * NB, 2 * NB)
        raw[:, pl.ds(at, 2 * NB)] = jnp.concatenate([pieces[d][0], pieces[d][1]], axis=1)
    raw_hi, raw_lo = split(raw[...])
    solved = []
    for n in range(0, size, wide):
        part = slice(0, n + wide)
        at = slice(n, n + wide)
        solved.append(
            dot3_nt(raw_hi[:, part], raw_lo[:, part], inv_hi_ref[0, at, part], inv_lo_ref[0, at, part])
        )
    solved_hi, solved_lo = split(jnp.concatenate(solved, axis=1))
    for n in range(0, size, wide):
        at = slice(n, n + wide)
        out = dot3_nn(solved_hi[:, n:], solved_lo[:, n:], inv_hi_ref[0, n:, at], inv_lo_ref[0, n:, at])
        for q in range(2):
            k = n // NB + q
            into = slice((k // 2) * NB, (k // 2 + 1) * NB)
            hi_ref[k % 2, :, into], lo_ref[k % 2, :, into] = split(out[:, q * NB : (q + 1) * NB])


def solve_both(where, pieces, inv_hi, inv_lo, tile=320):
    fronts, size, _ = inv_hi.shape
    per = pieces[0].shape[1] // fronts
    tiles = per // tile
    inv_spec = pl.BlockSpec((1, size, size), lambda f, i, w: (f, 0, 0))
    out_spec = pl.BlockSpec((2, tile, RING * NB), lambda f, i, w: (f, i, 0))
    return pl.pallas_call(
        rows_kernel,
        grid_spec=pltpu.PrefetchScalarGridSpec(
            num_scalar_prefetch=1,
            grid=(fronts, tiles),
            in_specs=[pl.BlockSpec((2, tile, NB), lambda f, i, w: (0, f * tiles + i, 0))] * RING + [inv_spec] * 2,
            out_specs=[out_spec] * 2,
            scratch_shapes=[pltpu.VMEM((tile, size), F32)],
        ),
        out_shape=[jax.ShapeDtypeStruct((2 * fronts, per, RING * NB), BF16)] * 2,
        compiler_params=pltpu.CompilerParams(vmem_limit_bytes=60 << 20),
        name="solve_both",
        cost_estimate=pl.CostEstimate(flops=12_000_000_000, bytes_accessed=18 << 20, transcendentals=0),
    )(where, *pieces, inv_hi, inv_lo)


def gather_rows(source, index_ref, base, width):
    sub = lax.broadcasted_iota(jnp.int32, (8, width), 0)
    picked = None
    for r in range(8):
        row = jnp.broadcast_to(source[pl.ds(index_ref[base + r], 1), :], (8, width))
        picked = row if picked is None else jnp.where(sub == r, row, picked)
    return picked


def product_kernel(where_ref, order_ref, *refs):
    split_z = len(refs[: -8]) == RING
    sides = refs[:-8]
    hi_ref, lo_ref, inv_hi_ref, inv_lo_ref, window_ref, out_ref, border_ref, updated = refs[-8:]
    low, z = where_ref[1] % 2, where_ref[1] // 2

    def lanes(k):
        return pl.ds(pl.multiple_of(k * NB, NB), NB)

    total, border = None, None
    for at in range(2):
        if split_z:
            order = [(z + RING - d) % RING for d in range(RING)]
            c_hi, c_lo = split(jnp.concatenate([side[at] for side in sides], axis=1))
            t_hi = jnp.concatenate([hi_ref[at, :, lanes(k)] for k in order], axis=1)
            t_lo = jnp.concatenate([lo_ref[at, :, lanes(k)] for k in order], axis=1)
            which = [2 * k + at for k in order]
        else:
            own = (low + at) % 2
            c_hi, c_lo = split(jnp.concatenate([sides[at][k] for k in range(RING)], axis=1))
            t_hi, t_lo = hi_ref[own], lo_ref[own]
            which = [2 * k + own for k in range(RING)]
        part = dot3_nt(t_hi, t_lo, c_hi, c_lo)
        w_hi = jnp.concatenate([inv_hi_ref[0, :, lanes(k)] for k in which], axis=1)
        w_lo = jnp.concatenate([inv_lo_ref[0, :, lanes(k)] for k in which], axis=1)
        piece = dot3_nt(c_hi, c_lo, w_hi, w_lo)
        total = part if total is None else total + part
        border = piece if border is None else border + piece
    border_ref[...] = border
    updated[...] = window_ref[...] - total
    width = out_ref.shape[1]

    def group(s, carry):
        for q in range(2):
            base = pl.multiple_of(s * 16 + q * 8, 8)
            out_ref[pl.ds(base, 8), :] = gather_rows(updated, order_ref, base, width)
        return carry

    lax.fori_loop(0, out_ref.shape[0] // 16, group, 0)


def product(where, order, sides, rows_hi, rows_lo, inv_hi, inv_lo, window, first, tile=256):
    _, rows, _ = rows_hi.shape
    size = inv_hi.shape[2]
    depth, tall, _ = sides[0].shape
    tiles = tall // tile
    rows_spec = pl.BlockSpec(rows_hi.shape, lambda i, w, o: (0, 0, 0), pipeline_mode=pl.Buffered(1))
    inv_spec = pl.BlockSpec((1, NB, size), lambda i, w, o: (0, w[1], 0), pipeline_mode=pl.Buffered(1))
    return pl.pallas_call(
        product_kernel,
        grid_spec=pltpu.PrefetchScalarGridSpec(
            num_scalar_prefetch=2,
            grid=(tiles,),
            in_specs=[pl.BlockSpec((depth, tile, NB), lambda i, w, o: (0, i, 0))] * len(sides)
            + [rows_spec] * 2
            + [inv_spec] * 2
            + [pl.BlockSpec((rows, tile), lambda i, w, o: (0, first * tiles + i))],
            out_specs=[
                pl.BlockSpec((rows, tile), lambda i, w, o: (0, i)),
                pl.BlockSpec((tile, NB), lambda i, w, o: (i, 0)),
            ],
            scratch_shapes=[pltpu.VMEM((rows, tile), F32)],
        ),
        out_shape=[jax.ShapeDtypeStruct((rows, tall), F32), jax.ShapeDtypeStruct((tall, NB), F32)],
        compiler_params=pltpu.CompilerParams(vmem_limit_bytes=60 << 20),
        name="product",
        cost_estimate=pl.CostEstimate(flops=9_000_000_000, bytes_accessed=20 << 20, transcendentals=0),
    )(where, order, *sides, rows_hi, rows_lo, inv_hi, inv_lo, window)


def assemble_kernel(first_ref, second_ref, arrived_ref, *refs):
    out_ref = refs[-1]
    per, width = out_ref.shape

    def group(s, carry):
        for q in range(2):
            base = pl.multiple_of(s * 16 + q * 8, 8)
            out_ref[pl.ds(base, 8), :] = gather_rows(arrived_ref, first_ref, base, width) + gather_rows(
                arrived_ref, second_ref, base, width
            )
        return carry

    lax.fori_loop(0, per // 16, group, 0)


def assemble(place, arrived, parent, first, width, tile=256):
    total, cols = arrived.shape
    per = place.shape[0] // 2
    tiles = cols // tile
    extra = [] if parent is None else [parent]
    return pl.pallas_call(
        assemble_kernel,
        grid_spec=pltpu.PrefetchScalarGridSpec(
            num_scalar_prefetch=2,
            grid=(tiles,),
            in_specs=[pl.BlockSpec((total, tile), lambda i, p, q: (0, i))]
            + [pl.BlockSpec(memory_space=pl.ANY)] * len(extra),
            out_specs=pl.BlockSpec((per, tile), lambda i, p, q: (0, first * tiles + i)),
        ),
        out_shape=jax.ShapeDtypeStruct((per, width), F32),
        input_output_aliases={3: 0} if extra else {},
        compiler_params=pltpu.CompilerParams(vmem_limit_bytes=60 << 20),
        name="assemble",
        cost_estimate=pl.CostEstimate(flops=4_000_000, bytes_accessed=8 << 20, transcendentals=0),
    )(place[:per], place[per:], arrived, *extra)


def per_device(pivot_panel, border_panel, window, assembly_map):
    front = lax.axis_index("sub")
    row_index = lax.axis_index("row")
    col_index = lax.axis_index("col")
    fronts, n_row, n_col = lax.axis_size("sub"), lax.axis_size("row"), lax.axis_size("col")
    pivot_local, border_local, window_local = pivot_panel[0], border_panel[0], window[0]
    size = n_row * pivot_local.shape[0]
    rows_kept, width = window_local.shape
    groups = fronts * n_row
    per = rows_kept // fronts
    capacity = rows_kept // groups
    both = ("sub", "row")
    where = jnp.stack([front, row_index, col_index])

    def exchange(x):
        return lax.all_to_all(x, both, split_axis=0, concat_axis=0, tiled=True)

    pivots, half_a, half_b, rows = exchange_all(pivot_local, border_local, rows_kept)

    beside = [(r, r ^ 1) for r in range(n_row)]
    side_a = [half_a, lax.ppermute(half_a, "row", beside)]
    side_b = [half_b]
    pieces = [rows]
    for d in (1, 2, 3):
        side_b.append(lax.ppermute(half_b, "row", [(r, (r + 2 * d) % n_row) for r in range(n_row)]))
        pieces.append(lax.ppermute(rows, "col", [(c, (c + 2 * d) % n_col) for c in range(n_col)]))

    inv_hi, inv_lo, pivot_factor = factor_fronts(where, pivots, 1, size)

    targets, ordering = lax.sort((assembly_map[0], lax.iota(jnp.int32, rows_kept)), num_keys=1)
    slots = exchange((targets % per).reshape(groups, capacity)).reshape(-1)
    owner = lax.iota(jnp.int32, rows_kept) // per
    _, place = lax.sort((slots + owner * per, lax.iota(jnp.int32, rows_kept)), num_keys=1)

    rows_hi, rows_lo = solve_both(where, pieces, inv_hi, inv_lo)
    side_a, side_b = lax.optimization_barrier((side_a, side_b))
    turn = [(r * n_col + c, c * n_row + r) for r in range(n_row) for c in range(n_col)]
    parent, border_halves = None, []
    arrived = []
    for first, sides in enumerate((side_a, side_b)):
        sent, turned = product(where, ordering, sides, rows_hi, rows_lo, inv_hi, inv_lo, window_local, first)
        border_halves.append(turned)
        arrived.append(exchange(sent.reshape(groups, capacity, -1)).reshape(rows_kept, -1))
    border_factor = lax.ppermute(jnp.concatenate(border_halves, axis=0), ("row", "col"), turn)
    for first in range(2):
        parent = assemble(place, arrived[first], parent, first, width)
    return (pivot_factor[None], border_factor[None], parent)


def solution(mesh):
    in_specs = (
        P("sub", "row", "col"),
        P("sub", "row", "col"),
        P("sub", "row", "col"),
        P("sub", "row"),
    )
    out_specs = (P("sub", "row", "col"), P("sub", "row", "col"), P(("sub", "row"), "col"))
    return jax.shard_map(
        per_device, mesh=mesh, in_specs=in_specs, out_specs=out_specs, check_vma=False
    )
```

```python
import functools

import jax
import jax.numpy as jnp
from jax import lax
from jax.experimental import pallas as pl
from jax.experimental.pallas import tpu as pltpu
from jax.sharding import PartitionSpec as P

NB = 128
F32 = jnp.float32
BF16 = jnp.bfloat16


def split(x):
    hi = x.astype(BF16)
    return hi, (x - hi.astype(F32)).astype(BF16)


def dot_nn(a, b):
    return lax.dot_general(a, b, (((1,), (0,)), ((), ())), preferred_element_type=F32)


def dot_nt(a, b):
    return lax.dot_general(a, b, (((1,), (1,)), ((), ())), preferred_element_type=F32)


def dot3_nn(a_hi, a_lo, b_hi, b_lo):
    return dot_nn(jnp.concatenate([a_hi, a_lo, a_hi], axis=1), jnp.concatenate([b_hi, b_hi, b_lo], axis=0))


def dot3_nt(a_hi, a_lo, b_hi, b_lo):
    return dot_nt(jnp.concatenate([a_hi, a_lo, a_hi], axis=1), jnp.concatenate([b_hi, b_hi, b_lo], axis=1))


def eliminate(blocks):
    lane = lax.broadcasted_iota(jnp.int32, (8, NB), 1)
    sub = lax.broadcasted_iota(jnp.int32, (8, NB), 0)
    shape = (8, NB)
    for g in range(NB // 8):
        first = 8 * g
        for block in blocks:
            rows = [jnp.broadcast_to(block[g][k : k + 1, :], shape) for k in range(8)]
            scalar = {
                (k, n): jnp.broadcast_to(rows[k][:, first + n : first + n + 1], shape)
                for k in range(8)
                for n in range(k, 8)
            }
            inverse, factor = [], {}
            for k in range(8):
                inv = 1.0 / scalar[k, k]
                inverse.append(inv)
                unit = jnp.where(lane == first + k, 1.0, rows[k])
                for n in range(k + 1, 8):
                    m = scalar[k, n] * inv
                    factor[k, n] = m
                    for q in range(n, 8):
                        scalar[n, q] = scalar[n, q] - m * scalar[k, q]
                    rows[n] = jnp.where(lane == first + k, 0.0, rows[n]) - m * unit
            scaled = []
            for k in range(8):
                hat = jnp.where(lane == first + k, 1.0, rows[k])
                if k < 7:
                    hat = jnp.where(jnp.logical_and(lane > first + k, lane < first + 8), 0.0, hat)
                scaled.append(hat * inverse[k])
            for i in range(g + 1, NB // 8):
                column = [jnp.broadcast_to(block[i][:, first + k : first + k + 1], shape) for k in range(8)]
                for k in range(8):
                    for n in range(k + 1, 8):
                        column[n] = column[n] - column[k] * factor[k, n]
                inside = jnp.logical_and(lane >= first, lane < first + 8)
                rest = jnp.where(inside, 0.0, block[i])
                even = column[0] * scaled[0]
                odd = column[1] * scaled[1]
                for k in range(2, 8, 2):
                    even = even + column[k] * scaled[k]
                    odd = odd + column[k + 1] * scaled[k + 1]
                block[i] = rest - (even + odd)
            own = rows[0]
            for k in range(1, 8):
                own = jnp.where(sub == k, rows[k], own)
            block[g] = own
    return blocks


def factor_kernel(where_ref, pivot_ref, hi_ref, lo_ref, factor_ref, work, panel):
    fronts = work.shape[0]
    size = work.shape[1]
    steps = size // NB
    row_at, col_at = where_ref[1], where_ref[2]
    for f in range(fronts):
        for r in range(steps):
            for c in range(steps):
                work[f, r * NB : (r + 1) * NB, c * NB : (c + 1) * NB] = pivot_ref[c % 2, c // 2, r // 2, r % 2]
    lane = lax.broadcasted_iota(jnp.int32, (NB, NB), 1)
    sub = lax.broadcasted_iota(jnp.int32, (NB, NB), 0)
    factor_ref[...] = jnp.zeros_like(factor_ref)

    def step(j, carry):
        base = pl.multiple_of(j * NB, NB)
        here = pl.ds(base, NB)
        blocks = []
        for f in range(fronts):
            blocks.append([work[f, pl.ds(base + 8 * i, 8), here] for i in range(NB // 8)])
        blocks = eliminate(blocks)
        columns = lax.broadcasted_iota(jnp.int32, (NB, size), 1)
        rows = lax.broadcasted_iota(jnp.int32, (size, NB), 0)
        for f in range(fronts):
            done = jnp.concatenate(blocks[f], axis=0)
            diag = jnp.sum(jnp.where(lane == sub, done, 0.0), axis=1, keepdims=True)
            scale = lax.rsqrt(diag)
            inverse = jnp.where(lane < sub, done, jnp.where(lane == sub, 1.0, 0.0)) * scale
            upper = jnp.where(lane >= sub, done, 0.0) * scale
            inv_hi, inv_lo = split(inverse)
            below_hi, below_lo = split(work[f, :, here])
            left = dot3_nt(below_hi, below_lo, inv_hi, inv_lo)
            left = jnp.where(rows >= base + NB, left, 0.0)
            panel[f] = left
            work[f, here, here] = jnp.zeros((NB, NB), F32)
            right_hi, right_lo = split(work[f, here, :])
            right = dot3_nn(inv_hi, inv_lo, right_hi, right_lo)
            work[f, here, :] = right
            work[f, here, here] = inverse
            full = work[f, here, :]
            lower = jnp.where(columns < base + NB, full, 0.0)
            low_hi, low_lo = split(lower)
            hi_ref[f, here, :] = low_hi
            lo_ref[f, here, :] = low_lo
            full_hi, full_lo = split(full)
            stacked = jnp.concatenate([full_hi, full_hi, full_lo], axis=0)

            @pl.when(j == col_at)
            def _():
                factor_ref[...] = jnp.where(
                    row_at == j, upper.T, panel[f, pl.ds(pl.multiple_of(row_at * NB, NB), NB), :]
                )

            def trail(i, carry):
                at = pl.ds(pl.multiple_of(i * NB, NB), NB)
                work[f, at, here] = jnp.zeros((NB, NB), F32)
                l_hi, l_lo = split(panel[f, at, :])
                work[f, at, :] -= dot_nn(jnp.concatenate([l_hi, l_lo, l_hi], axis=1), stacked)
                return carry

            lax.fori_loop(j + 1, steps, trail, 0)
        return carry

    lax.fori_loop(0, steps, step, 0)


def factor_fronts(where, pivots, fronts, size):
    return pl.pallas_call(
        factor_kernel,
        in_specs=[pl.BlockSpec(memory_space=pltpu.SMEM), pl.BlockSpec(memory_space=pltpu.VMEM)],
        out_specs=[pl.BlockSpec(memory_space=pltpu.VMEM)] * 3,
        out_shape=[
            jax.ShapeDtypeStruct((fronts, size, size), BF16),
            jax.ShapeDtypeStruct((fronts, size, size), BF16),
            jax.ShapeDtypeStruct((NB, NB), F32),
        ],
        scratch_shapes=[pltpu.VMEM((fronts, size, size), F32), pltpu.VMEM((fronts, size, NB), F32)],
        compiler_params=pltpu.CompilerParams(vmem_limit_bytes=60 << 20),
        name="factor_fronts",
        cost_estimate=pl.CostEstimate(flops=20_000_000_000, bytes_accessed=16 << 20, transcendentals=0),
    )(where, pivots)


MESH = pl.DeviceIdType.MESH
RING = 4


def exchange_kernel(
    pivot_ref, border_ref, slots_ref, pivots, half_a, half_b, rows_out, slots_out, send, recv, local
):
    s, r, c = lax.axis_index("sub"), lax.axis_index("row"), lax.axis_index("col")
    low, z, y, core = r % 2, r // 2, c // 2, c % 2

    def device(low, y, z, core):
        return {"sub": s, "row": 2 * z + low, "col": 2 * y + core}

    along_y = [device(low, (y + d) % RING, z, core) for d in (1, 2, 3)]
    along_z = [device(low, y, (z + d) % RING, core) for d in (1, 2, 3)]
    beside = device(1 - low, y, z, core)
    mate = device(low, y, z, 1 - core)
    turned = {"sub": s, "row": c, "col": r}
    groups = slots_ref.shape[0]
    per_front = groups // 2
    group = s * per_front + r
    plane = [(group + o) % groups for o in range(1, groups)]
    spread_to = [{"sub": g // per_front, "row": g % per_front, "col": c} for g in plane]
    count = [0]

    def copy(src, dst, to):
        n = count[0]
        count[0] += 1
        return pltpu.make_async_remote_copy(
            src_ref=src, dst_ref=dst, send_sem=send.at[n], recv_sem=recv.at[n], device_id=to, device_id_type=MESH
        )

    barrier = pltpu.get_barrier_semaphore()
    peers = along_y + [mate] + spread_to
    for peer in peers:
        pl.semaphore_signal(barrier, inc=1, device_id=peer, device_id_type=MESH)

    @pl.when(r != c)
    def _():
        pl.semaphore_signal(barrier, inc=1, device_id=turned, device_id_type=MESH)

    pl.semaphore_wait(barrier, len(peers) + (r != c).astype(jnp.int32))

    tall = half_a.shape[1]
    kept = rows_out.shape[1]
    half = NB // 2
    one, two = pl.ds(0, half), pl.ds(half, half)

    first = [copy(pivot_ref.at[one], pivots.at[core, y, z, low, one], to) for to in along_z]
    first += [copy(pivot_ref.at[two], pivots.at[core, y, z, low, two], to) for to in along_y]
    for item in first:
        item.start()
    own = [
        pltpu.make_async_copy(pivot_ref, pivots.at[core, y, z, low], local.at[0]),
        pltpu.make_async_copy(border_ref.at[pl.ds(0, kept)], rows_out.at[core], local.at[1]),
    ]
    for item in own:
        item.start()
    swap_rows = copy(border_ref.at[pl.ds(0, kept)], rows_out.at[core], mate)
    swap_rows.start()
    turn_a = copy(border_ref.at[pl.ds(0, tall)], half_a.at[c // 2], turned)
    turn_b = copy(border_ref.at[pl.ds(tall, tall)], half_b.at[c % 2], turned)
    keep_a = pltpu.make_async_copy(border_ref.at[pl.ds(0, tall)], half_a.at[z], local.at[2])
    keep_b = pltpu.make_async_copy(border_ref.at[pl.ds(tall, tall)], half_b.at[low], local.at[3])

    @pl.when(r != c)
    def _():
        turn_a.start()
        turn_b.start()

    @pl.when(r == c)
    def _():
        keep_a.start()
        keep_b.start()

    keep_slots = pltpu.make_async_copy(slots_ref.at[group], slots_out.at[group], local.at[4])
    keep_slots.start()
    spread = [copy(slots_ref.at[g], slots_out.at[group], to) for g, to in zip(plane, spread_to)]
    for item in spread:
        item.start()

    own[0].wait()
    for item in first:
        item.wait_recv()
    area_one, area_two = pivots.at[core, y, :, low, one], pivots.at[core, :, z, low, two]
    second = [copy(area_one, area_one, beside), copy(area_two, area_two, beside)]
    for item in second:
        item.start()

    for item in second:
        item.wait_recv()
    area_one, area_two = pivots.at[core, y, :, :, one], pivots.at[core, :, z, :, two]
    third = [copy(area_one, area_one, to) for to in along_y]
    third += [copy(area_two, area_two, to) for to in along_z]
    swaps = [copy(area_one, area_one, mate), copy(area_two, area_two, mate)]
    for item in third + swaps:
        item.start()

    @pl.when(r != c)
    def _():
        turn_a.wait_recv()
        turn_b.wait_recv()

    @pl.when(r == c)
    def _():
        keep_a.wait()
        keep_b.wait()

    stage = [copy(half_a.at[z], half_a.at[z], to) for to in along_z]
    stage += [copy(half_b.at[low], half_b.at[low], beside)]
    for item in stage:
        item.start()
    for d in (1, 2, 3):
        third[d - 1].wait_recv()
        area = pivots.at[core, (y + RING - d) % RING, :, :, one]
        swaps.append(copy(area, area, mate))
        swaps[-1].start()
        third[d + 2].wait_recv()
        area = pivots.at[core, :, (z + RING - d) % RING, :, two]
        swaps.append(copy(area, area, mate))
        swaps[-1].start()

    own[1].wait()
    keep_slots.wait()
    for item in swaps + stage + spread + [swap_rows]:
        item.wait_recv()
    for item in first + second + third + swaps + stage + spread + [swap_rows]:
        item.wait_send()

    @pl.when(r != c)
    def _():
        turn_a.wait_send()
        turn_b.wait_send()


def exchange_all(pivot, border, slots, kept):
    tall = border.shape[0] // 2
    copies = 32 + slots.shape[0] - 1
    return pl.pallas_call(
        exchange_kernel,
        in_specs=[pl.BlockSpec(memory_space=pltpu.VMEM)] * 3,
        out_specs=[pl.BlockSpec(memory_space=pl.ANY)] * 5,
        out_shape=[
            jax.ShapeDtypeStruct((2, RING, RING, 2, NB, NB), F32),
            jax.ShapeDtypeStruct((RING, tall, NB), F32),
            jax.ShapeDtypeStruct((2, tall, NB), F32),
            jax.ShapeDtypeStruct((2, kept, NB), F32),
            jax.ShapeDtypeStruct(slots.shape, jnp.int32),
        ],
        scratch_shapes=[
            pltpu.SemaphoreType.DMA((copies,)),
            pltpu.SemaphoreType.DMA((copies,)),
            pltpu.SemaphoreType.DMA((5,)),
        ],
        compiler_params=pltpu.CompilerParams(
            collective_id=0, has_side_effects=True, vmem_limit_bytes=60 << 20
        ),
        name="exchange_all",
    )(pivot, border, slots)


def rows_kernel(where_ref, *refs):
    pieces, (inv_hi_ref, inv_lo_ref, hi_ref, lo_ref, raw) = refs[:RING], refs[RING:]
    size = inv_hi_ref.shape[2]
    y = where_ref[2] // 2
    wide = 256
    for d in range(RING):
        at = pl.multiple_of(((y + RING - d) % RING) * 2 * NB, 2 * NB)
        raw[:, pl.ds(at, 2 * NB)] = jnp.concatenate([pieces[d][0], pieces[d][1]], axis=1)
    raw_hi, raw_lo = split(raw[...])
    solved = []
    for n in range(0, size, wide):
        part = slice(0, n + wide)
        at = slice(n, n + wide)
        solved.append(
            dot3_nt(raw_hi[:, part], raw_lo[:, part], inv_hi_ref[0, at, part], inv_lo_ref[0, at, part])
        )
    solved_hi, solved_lo = split(jnp.concatenate(solved, axis=1))
    for n in range(0, size, wide):
        at = slice(n, n + wide)
        out = dot3_nn(solved_hi[:, n:], solved_lo[:, n:], inv_hi_ref[0, n:, at], inv_lo_ref[0, n:, at])
        for q in range(2):
            k = n // NB + q
            into = slice((k // 2) * NB, (k // 2 + 1) * NB)
            hi_ref[k % 2, :, into], lo_ref[k % 2, :, into] = split(out[:, q * NB : (q + 1) * NB])


def solve_both(where, pieces, inv_hi, inv_lo, tile=320):
    fronts, size, _ = inv_hi.shape
    per = pieces[0].shape[1] // fronts
    tiles = per // tile
    inv_spec = pl.BlockSpec((1, size, size), lambda f, i, w: (f, 0, 0))
    out_spec = pl.BlockSpec((2, tile, RING * NB), lambda f, i, w: (f, i, 0))
    return pl.pallas_call(
        rows_kernel,
        grid_spec=pltpu.PrefetchScalarGridSpec(
            num_scalar_prefetch=1,
            grid=(fronts, tiles),
            in_specs=[pl.BlockSpec((2, tile, NB), lambda f, i, w: (0, f * tiles + i, 0))] * RING + [inv_spec] * 2,
            out_specs=[out_spec] * 2,
            scratch_shapes=[pltpu.VMEM((tile, size), F32)],
        ),
        out_shape=[jax.ShapeDtypeStruct((2 * fronts, per, RING * NB), BF16)] * 2,
        compiler_params=pltpu.CompilerParams(vmem_limit_bytes=60 << 20),
        name="solve_both",
        cost_estimate=pl.CostEstimate(flops=12_000_000_000, bytes_accessed=18 << 20, transcendentals=0),
    )(where, *pieces, inv_hi, inv_lo)


def scatter_kernel(sent_ref, arrived_ref, send, recv, local):
    s, r, c = lax.axis_index("sub"), lax.axis_index("row"), lax.axis_index("col")
    groups = sent_ref.shape[0]
    per_front = groups // 2
    group = s * per_front + r
    others = [(group + o) % groups for o in range(1, groups)]
    where_to = [{"sub": g // per_front, "row": g % per_front, "col": c} for g in others]
    barrier = pltpu.get_barrier_semaphore()
    for to in where_to:
        pl.semaphore_signal(barrier, inc=1, device_id=to, device_id_type=MESH)
    pl.semaphore_wait(barrier, len(where_to))
    copies = [
        pltpu.make_async_remote_copy(
            src_ref=sent_ref.at[g],
            dst_ref=arrived_ref.at[group],
            send_sem=send.at[n],
            recv_sem=recv.at[n],
            device_id=to,
            device_id_type=MESH,
        )
        for n, (g, to) in enumerate(zip(others, where_to))
    ]
    for item in copies:
        item.start()
    keep = pltpu.make_async_copy(sent_ref.at[group], arrived_ref.at[group], local)
    keep.start()
    keep.wait()
    for item in copies:
        item.wait_recv()
    for item in copies:
        item.wait_send()


def scatter_rows(sent):
    others = sent.shape[0] - 1
    return pl.pallas_call(
        scatter_kernel,
        in_specs=[pl.BlockSpec(memory_space=pl.ANY)],
        out_specs=pl.BlockSpec(memory_space=pl.ANY),
        out_shape=jax.ShapeDtypeStruct(sent.shape, F32),
        scratch_shapes=[
            pltpu.SemaphoreType.DMA((others,)),
            pltpu.SemaphoreType.DMA((others,)),
            pltpu.SemaphoreType.DMA,
        ],
        compiler_params=pltpu.CompilerParams(
            collective_id=1, has_side_effects=True, vmem_limit_bytes=60 << 20
        ),
        name="scatter_rows",
    )(sent)


def gather_rows(source, index_ref, base, width):
    sub = lax.broadcasted_iota(jnp.int32, (8, width), 0)
    picked = None
    for r in range(8):
        row = jnp.broadcast_to(source[pl.ds(index_ref[base + r], 1), :], (8, width))
        picked = row if picked is None else jnp.where(sub == r, row, picked)
    return picked


def product_kernel(where_ref, order_ref, *refs):
    split_z = len(refs[: -8]) == RING
    sides = refs[:-8]
    hi_ref, lo_ref, inv_hi_ref, inv_lo_ref, window_ref, out_ref, border_ref, updated = refs[-8:]
    low, z = where_ref[1] % 2, where_ref[1] // 2

    def lanes(k):
        return pl.ds(pl.multiple_of(k * NB, NB), NB)

    total, border = None, None
    for at in range(2):
        if split_z:
            order = [(z + RING - d) % RING for d in range(RING)]
            c_hi, c_lo = split(jnp.concatenate([side[at] for side in sides], axis=1))
            t_hi = jnp.concatenate([hi_ref[at, :, lanes(k)] for k in order], axis=1)
            t_lo = jnp.concatenate([lo_ref[at, :, lanes(k)] for k in order], axis=1)
            which = [2 * k + at for k in order]
        else:
            own = (low + at) % 2
            c_hi, c_lo = split(jnp.concatenate([sides[at][k] for k in range(RING)], axis=1))
            t_hi, t_lo = hi_ref[own], lo_ref[own]
            which = [2 * k + own for k in range(RING)]
        part = dot3_nt(t_hi, t_lo, c_hi, c_lo)
        w_hi = jnp.concatenate([inv_hi_ref[0, :, lanes(k)] for k in which], axis=1)
        w_lo = jnp.concatenate([inv_lo_ref[0, :, lanes(k)] for k in which], axis=1)
        piece = dot3_nt(c_hi, c_lo, w_hi, w_lo)
        total = part if total is None else total + part
        border = piece if border is None else border + piece
    border_ref[...] = border
    updated[...] = window_ref[...] - total
    width = out_ref.shape[1]

    def group(s, carry):
        for q in range(2):
            base = pl.multiple_of(s * 16 + q * 8, 8)
            out_ref[pl.ds(base, 8), :] = gather_rows(updated, order_ref, base, width)
        return carry

    lax.fori_loop(0, out_ref.shape[0] // 16, group, 0)


def product(where, order, sides, rows_hi, rows_lo, inv_hi, inv_lo, window, first, tile=512):
    _, rows, _ = rows_hi.shape
    size = inv_hi.shape[2]
    depth, tall, _ = sides[0].shape
    tiles = tall // tile
    rows_spec = pl.BlockSpec(rows_hi.shape, lambda i, w, o: (0, 0, 0), pipeline_mode=pl.Buffered(1))
    inv_spec = pl.BlockSpec((1, NB, size), lambda i, w, o: (0, w[1], 0), pipeline_mode=pl.Buffered(1))
    return pl.pallas_call(
        product_kernel,
        grid_spec=pltpu.PrefetchScalarGridSpec(
            num_scalar_prefetch=2,
            grid=(tiles,),
            in_specs=[pl.BlockSpec((depth, tile, NB), lambda i, w, o: (0, i, 0))] * len(sides)
            + [rows_spec] * 2
            + [inv_spec] * 2
            + [pl.BlockSpec((rows, tile), lambda i, w, o: (0, first * tiles + i))],
            out_specs=[
                pl.BlockSpec((rows, tile), lambda i, w, o: (0, i)),
                pl.BlockSpec((tile, NB), lambda i, w, o: (i, 0)),
            ],
            scratch_shapes=[pltpu.VMEM((rows, tile), F32)],
        ),
        out_shape=[jax.ShapeDtypeStruct((rows, tall), F32), jax.ShapeDtypeStruct((tall, NB), F32)],
        compiler_params=pltpu.CompilerParams(vmem_limit_bytes=60 << 20),
        name="product",
        cost_estimate=pl.CostEstimate(flops=9_000_000_000, bytes_accessed=20 << 20, transcendentals=0),
    )(where, order, *sides, rows_hi, rows_lo, inv_hi, inv_lo, window)


def assemble_kernel(first_ref, second_ref, arrived_ref, *refs):
    out_ref = refs[-1]
    per, width = out_ref.shape

    def group(s, carry):
        for q in range(2):
            base = pl.multiple_of(s * 16 + q * 8, 8)
            out_ref[pl.ds(base, 8), :] = gather_rows(arrived_ref, first_ref, base, width) + gather_rows(
                arrived_ref, second_ref, base, width
            )
        return carry

    lax.fori_loop(0, per // 16, group, 0)


def assemble(place, arrived, parent, first, width, tile=512):
    total, cols = arrived.shape
    per = place.shape[0] // 2
    tiles = cols // tile
    extra = [] if parent is None else [parent]
    return pl.pallas_call(
        assemble_kernel,
        grid_spec=pltpu.PrefetchScalarGridSpec(
            num_scalar_prefetch=2,
            grid=(tiles,),
            in_specs=[pl.BlockSpec((total, tile), lambda i, p, q: (0, i))]
            + [pl.BlockSpec(memory_space=pl.ANY)] * len(extra),
            out_specs=pl.BlockSpec((per, tile), lambda i, p, q: (0, first * tiles + i)),
        ),
        out_shape=jax.ShapeDtypeStruct((per, width), F32),
        input_output_aliases={3: 0} if extra else {},
        compiler_params=pltpu.CompilerParams(vmem_limit_bytes=60 << 20),
        name="assemble",
        cost_estimate=pl.CostEstimate(flops=4_000_000, bytes_accessed=8 << 20, transcendentals=0),
    )(place[:per], place[per:], arrived, *extra)


def per_device(pivot_panel, border_panel, window, assembly_map):
    front = lax.axis_index("sub")
    row_index = lax.axis_index("row")
    col_index = lax.axis_index("col")
    fronts, n_row, n_col = lax.axis_size("sub"), lax.axis_size("row"), lax.axis_size("col")
    pivot_local, border_local, window_local = pivot_panel[0], border_panel[0], window[0]
    size = n_row * pivot_local.shape[0]
    rows_kept, width = window_local.shape
    groups = fronts * n_row
    per = rows_kept // fronts
    capacity = rows_kept // groups
    both = ("sub", "row")
    where = jnp.stack([front, row_index, col_index])

    def exchange(x):
        return lax.all_to_all(x, both, split_axis=0, concat_axis=0, tiled=True)

    targets, ordering = lax.sort((assembly_map[0], lax.iota(jnp.int32, rows_kept)), num_keys=1)
    slots = jnp.pad((targets % per).reshape(groups, 1, capacity), ((0, 0), (0, 7), (0, NB - capacity)))
    pivots, half_a, half_b, rows, slots = exchange_all(pivot_local, border_local, slots, rows_kept)

    beside = [(r, r ^ 1) for r in range(n_row)]
    side_a = [half_a, lax.ppermute(half_a, "row", beside)]
    side_b = [half_b]
    pieces = [rows]
    for d in (1, 2, 3):
        side_b.append(lax.ppermute(half_b, "row", [(r, (r + 2 * d) % n_row) for r in range(n_row)]))
        pieces.append(lax.ppermute(rows, "col", [(c, (c + 2 * d) % n_col) for c in range(n_col)]))

    inv_hi, inv_lo, pivot_factor = factor_fronts(where, pivots, 1, size)

    owner = lax.iota(jnp.int32, rows_kept) // per
    _, place = lax.sort(
        (slots[:, 0, :capacity].reshape(-1) + owner * per, lax.iota(jnp.int32, rows_kept)), num_keys=1
    )

    rows_hi, rows_lo = solve_both(where, pieces, inv_hi, inv_lo)
    side_a, side_b = lax.optimization_barrier((side_a, side_b))
    turn = [(r * n_col + c, c * n_row + r) for r in range(n_row) for c in range(n_col)]
    parent, border_halves = None, []
    arrived = []
    for first, sides in enumerate((side_a, side_b)):
        sent, turned = product(where, ordering, sides, rows_hi, rows_lo, inv_hi, inv_lo, window_local, first)
        border_halves.append(turned)
        move = exchange if first == 0 else scatter_rows
        arrived.append(move(sent.reshape(groups, capacity, -1)).reshape(rows_kept, -1))
    border_factor = lax.ppermute(jnp.concatenate(border_halves, axis=0), ("row", "col"), turn)
    for first in range(2):
        parent = assemble(place, arrived[first], parent, first, width)
    return (pivot_factor[None], border_factor[None], parent)


def solution(mesh):
    in_specs = (
        P("sub", "row", "col"),
        P("sub", "row", "col"),
        P("sub", "row", "col"),
        P("sub", "row"),
    )
    out_specs = (P("sub", "row", "col"), P("sub", "row", "col"), P(("sub", "row"), "col"))
    return jax.shard_map(
        per_device, mesh=mesh, in_specs=in_specs, out_specs=out_specs, check_vma=False
    )
```

```python
import functools

import jax
import jax.numpy as jnp
from jax import lax
from jax.experimental import pallas as pl
from jax.experimental.pallas import tpu as pltpu
from jax.sharding import PartitionSpec as P

NB = 128
F32 = jnp.float32
BF16 = jnp.bfloat16


def split(x):
    hi = x.astype(BF16)
    return hi, (x - hi.astype(F32)).astype(BF16)


def dot_nn(a, b):
    return lax.dot_general(a, b, (((1,), (0,)), ((), ())), preferred_element_type=F32)


def dot_nt(a, b):
    return lax.dot_general(a, b, (((1,), (1,)), ((), ())), preferred_element_type=F32)


def dot3_nn(a_hi, a_lo, b_hi, b_lo):
    return dot_nn(jnp.concatenate([a_hi, a_lo, a_hi], axis=1), jnp.concatenate([b_hi, b_hi, b_lo], axis=0))


def dot3_nt(a_hi, a_lo, b_hi, b_lo):
    return dot_nt(jnp.concatenate([a_hi, a_lo, a_hi], axis=1), jnp.concatenate([b_hi, b_hi, b_lo], axis=1))


def eliminate(blocks):
    lane = lax.broadcasted_iota(jnp.int32, (8, NB), 1)
    sub = lax.broadcasted_iota(jnp.int32, (8, NB), 0)
    shape = (8, NB)
    for g in range(NB // 8):
        first = 8 * g
        for block in blocks:
            rows = [jnp.broadcast_to(block[g][k : k + 1, :], shape) for k in range(8)]
            scalar = {
                (k, n): jnp.broadcast_to(rows[k][:, first + n : first + n + 1], shape)
                for k in range(8)
                for n in range(k, 8)
            }
            inverse, factor = [], {}
            for k in range(8):
                inv = 1.0 / scalar[k, k]
                inverse.append(inv)
                unit = jnp.where(lane == first + k, 1.0, rows[k])
                for n in range(k + 1, 8):
                    m = scalar[k, n] * inv
                    factor[k, n] = m
                    for q in range(n, 8):
                        scalar[n, q] = scalar[n, q] - m * scalar[k, q]
                    rows[n] = jnp.where(lane == first + k, 0.0, rows[n]) - m * unit
            scaled = []
            for k in range(8):
                hat = jnp.where(lane == first + k, 1.0, rows[k])
                if k < 7:
                    hat = jnp.where(jnp.logical_and(lane > first + k, lane < first + 8), 0.0, hat)
                scaled.append(hat * inverse[k])
            for i in range(g + 1, NB // 8):
                column = [jnp.broadcast_to(block[i][:, first + k : first + k + 1], shape) for k in range(8)]
                for k in range(8):
                    for n in range(k + 1, 8):
                        column[n] = column[n] - column[k] * factor[k, n]
                inside = jnp.logical_and(lane >= first, lane < first + 8)
                rest = jnp.where(inside, 0.0, block[i])
                even = column[0] * scaled[0]
                odd = column[1] * scaled[1]
                for k in range(2, 8, 2):
                    even = even + column[k] * scaled[k]
                    odd = odd + column[k + 1] * scaled[k + 1]
                block[i] = rest - (even + odd)
            own = rows[0]
            for k in range(1, 8):
                own = jnp.where(sub == k, rows[k], own)
            block[g] = own
    return blocks


def factor_kernel(where_ref, pivot_ref, hi_ref, lo_ref, factor_ref, work, panel):
    fronts = work.shape[0]
    size = work.shape[1]
    steps = size // NB
    row_at, col_at = where_ref[1], where_ref[2]
    for f in range(fronts):
        for r in range(steps):
            for c in range(steps):
                work[f, r * NB : (r + 1) * NB, c * NB : (c + 1) * NB] = pivot_ref[c % 2, c // 2, r // 2, r % 2]
    lane = lax.broadcasted_iota(jnp.int32, (NB, NB), 1)
    sub = lax.broadcasted_iota(jnp.int32, (NB, NB), 0)
    factor_ref[...] = jnp.zeros_like(factor_ref)

    def step(j, carry):
        base = pl.multiple_of(j * NB, NB)
        here = pl.ds(base, NB)
        blocks = []
        for f in range(fronts):
            blocks.append([work[f, pl.ds(base + 8 * i, 8), here] for i in range(NB // 8)])
        blocks = eliminate(blocks)
        columns = lax.broadcasted_iota(jnp.int32, (NB, size), 1)
        rows = lax.broadcasted_iota(jnp.int32, (size, NB), 0)
        for f in range(fronts):
            done = jnp.concatenate(blocks[f], axis=0)
            diag = jnp.sum(jnp.where(lane == sub, done, 0.0), axis=1, keepdims=True)
            scale = lax.rsqrt(diag)
            inverse = jnp.where(lane < sub, done, jnp.where(lane == sub, 1.0, 0.0)) * scale
            upper = jnp.where(lane >= sub, done, 0.0) * scale
            inv_hi, inv_lo = split(inverse)
            below_hi, below_lo = split(work[f, :, here])
            left = dot3_nt(below_hi, below_lo, inv_hi, inv_lo)
            left = jnp.where(rows >= base + NB, left, 0.0)
            panel[f] = left
            work[f, here, here] = jnp.zeros((NB, NB), F32)
            right_hi, right_lo = split(work[f, here, :])
            right = dot3_nn(inv_hi, inv_lo, right_hi, right_lo)
            work[f, here, :] = right
            work[f, here, here] = inverse
            full = work[f, here, :]
            lower = jnp.where(columns < base + NB, full, 0.0)
            low_hi, low_lo = split(lower)
            hi_ref[f, here, :] = low_hi
            lo_ref[f, here, :] = low_lo
            full_hi, full_lo = split(full)
            stacked = jnp.concatenate([full_hi, full_hi, full_lo], axis=0)

            @pl.when(j == col_at)
            def _():
                factor_ref[...] = jnp.where(
                    row_at == j, upper.T, panel[f, pl.ds(pl.multiple_of(row_at * NB, NB), NB), :]
                )

            def trail(i, carry):
                at = pl.ds(pl.multiple_of(i * NB, NB), NB)
                work[f, at, here] = jnp.zeros((NB, NB), F32)
                l_hi, l_lo = split(panel[f, at, :])
                work[f, at, :] -= dot_nn(jnp.concatenate([l_hi, l_lo, l_hi], axis=1), stacked)
                return carry

            lax.fori_loop(j + 1, steps, trail, 0)
        return carry

    lax.fori_loop(0, steps, step, 0)


def factor_fronts(where, pivots, fronts, size):
    return pl.pallas_call(
        factor_kernel,
        in_specs=[pl.BlockSpec(memory_space=pltpu.SMEM), pl.BlockSpec(memory_space=pltpu.VMEM)],
        out_specs=[pl.BlockSpec(memory_space=pltpu.VMEM)] * 3,
        out_shape=[
            jax.ShapeDtypeStruct((fronts, size, size), BF16),
            jax.ShapeDtypeStruct((fronts, size, size), BF16),
            jax.ShapeDtypeStruct((NB, NB), F32),
        ],
        scratch_shapes=[pltpu.VMEM((fronts, size, size), F32), pltpu.VMEM((fronts, size, NB), F32)],
        compiler_params=pltpu.CompilerParams(vmem_limit_bytes=60 << 20),
        name="factor_fronts",
        cost_estimate=pl.CostEstimate(flops=20_000_000_000, bytes_accessed=16 << 20, transcendentals=0),
    )(where, pivots)


MESH = pl.DeviceIdType.MESH
RING = 4


def exchange_kernel(
    pivot_ref, border_ref, slots_ref, pivots, half_a, half_b, rows_out, rest_out, slots_out, send, recv, local
):
    s, r, c = lax.axis_index("sub"), lax.axis_index("row"), lax.axis_index("col")
    low, z, y, core = r % 2, r // 2, c // 2, c % 2

    def device(low, y, z, core):
        return {"sub": s, "row": 2 * z + low, "col": 2 * y + core}

    along_y = [device(low, (y + d) % RING, z, core) for d in (1, 2, 3)]
    along_z = [device(low, y, (z + d) % RING, core) for d in (1, 2, 3)]
    beside = device(1 - low, y, z, core)
    mate = device(low, y, z, 1 - core)
    turned = {"sub": s, "row": c, "col": r}
    groups = slots_ref.shape[0]
    per_front = groups // 2
    group = s * per_front + r
    plane = [(group + o) % groups for o in range(1, groups)]
    spread_to = [{"sub": g // per_front, "row": g % per_front, "col": c} for g in plane]
    count = [0]

    def copy(src, dst, to):
        n = count[0]
        count[0] += 1
        return pltpu.make_async_remote_copy(
            src_ref=src, dst_ref=dst, send_sem=send.at[n], recv_sem=recv.at[n], device_id=to, device_id_type=MESH
        )

    barrier = pltpu.get_barrier_semaphore()
    peers = along_y + [mate] + spread_to
    for peer in peers:
        pl.semaphore_signal(barrier, inc=1, device_id=peer, device_id_type=MESH)

    @pl.when(r != c)
    def _():
        pl.semaphore_signal(barrier, inc=1, device_id=turned, device_id_type=MESH)

    pl.semaphore_wait(barrier, len(peers) + (r != c).astype(jnp.int32))

    tall = half_a.shape[1]
    kept = rows_out.shape[1]
    rest = rest_out.shape[1]
    half = NB // 2
    one, two = pl.ds(0, half), pl.ds(half, half)

    first = [copy(pivot_ref.at[one], pivots.at[core, y, z, low, one], to) for to in along_z]
    first += [copy(pivot_ref.at[two], pivots.at[core, y, z, low, two], to) for to in along_y]
    for item in first:
        item.start()
    own = [
        pltpu.make_async_copy(pivot_ref, pivots.at[core, y, z, low], local.at[0]),
        pltpu.make_async_copy(border_ref.at[pl.ds(0, kept)], rows_out.at[core], local.at[1]),
        pltpu.make_async_copy(border_ref.at[pl.ds(kept, rest)], rest_out.at[core], local.at[5]),
    ]
    for item in own:
        item.start()
    swap_rows = copy(border_ref.at[pl.ds(0, kept)], rows_out.at[core], mate)
    swap_rest = copy(border_ref.at[pl.ds(kept, rest)], rest_out.at[core], mate)
    swap_rows.start()
    swap_rest.start()
    turn_a = copy(border_ref.at[pl.ds(0, tall)], half_a.at[c // 2], turned)
    turn_b = copy(border_ref.at[pl.ds(tall, tall)], half_b.at[c % 2], turned)
    keep_a = pltpu.make_async_copy(border_ref.at[pl.ds(0, tall)], half_a.at[z], local.at[2])
    keep_b = pltpu.make_async_copy(border_ref.at[pl.ds(tall, tall)], half_b.at[low], local.at[3])

    @pl.when(r != c)
    def _():
        turn_a.start()
        turn_b.start()

    @pl.when(r == c)
    def _():
        keep_a.start()
        keep_b.start()

    keep_slots = pltpu.make_async_copy(slots_ref.at[group], slots_out.at[group], local.at[4])
    keep_slots.start()
    spread = [copy(slots_ref.at[g], slots_out.at[group], to) for g, to in zip(plane, spread_to)]
    for item in spread:
        item.start()

    own[0].wait()
    for item in first:
        item.wait_recv()
    area_one, area_two = pivots.at[core, y, :, low, one], pivots.at[core, :, z, low, two]
    second = [copy(area_one, area_one, beside), copy(area_two, area_two, beside)]
    for item in second:
        item.start()

    for item in second:
        item.wait_recv()
    area_one, area_two = pivots.at[core, y, :, :, one], pivots.at[core, :, z, :, two]
    third = [copy(area_one, area_one, to) for to in along_y]
    third += [copy(area_two, area_two, to) for to in along_z]
    swaps = [copy(area_one, area_one, mate), copy(area_two, area_two, mate)]
    for item in third + swaps:
        item.start()

    @pl.when(r != c)
    def _():
        turn_a.wait_recv()
        turn_b.wait_recv()

    @pl.when(r == c)
    def _():
        keep_a.wait()
        keep_b.wait()

    stage = [copy(half_a.at[z], half_a.at[z], to) for to in along_z]
    stage += [copy(half_b.at[low], half_b.at[low], beside)]
    for item in stage:
        item.start()
    for d in (1, 2, 3):
        third[d - 1].wait_recv()
        area = pivots.at[core, (y + RING - d) % RING, :, :, one]
        swaps.append(copy(area, area, mate))
        swaps[-1].start()
        third[d + 2].wait_recv()
        area = pivots.at[core, :, (z + RING - d) % RING, :, two]
        swaps.append(copy(area, area, mate))
        swaps[-1].start()

    own[1].wait()
    own[2].wait()
    keep_slots.wait()
    for item in swaps + stage + spread + [swap_rows, swap_rest]:
        item.wait_recv()
    for item in first + second + third + swaps + stage + spread + [swap_rows, swap_rest]:
        item.wait_send()

    @pl.when(r != c)
    def _():
        turn_a.wait_send()
        turn_b.wait_send()


def exchange_all(pivot, border, slots, kept):
    tall = border.shape[0] // 2
    copies = 33 + slots.shape[0] - 1
    return pl.pallas_call(
        exchange_kernel,
        in_specs=[pl.BlockSpec(memory_space=pltpu.VMEM)] * 3,
        out_specs=[pl.BlockSpec(memory_space=pl.ANY)] * 6,
        out_shape=[
            jax.ShapeDtypeStruct((2, RING, RING, 2, NB, NB), F32),
            jax.ShapeDtypeStruct((RING, tall, NB), F32),
            jax.ShapeDtypeStruct((2, tall, NB), F32),
            jax.ShapeDtypeStruct((2, kept, NB), F32),
            jax.ShapeDtypeStruct((2, border.shape[0] - kept, NB), F32),
            jax.ShapeDtypeStruct(slots.shape, jnp.int32),
        ],
        scratch_shapes=[
            pltpu.SemaphoreType.DMA((copies,)),
            pltpu.SemaphoreType.DMA((copies,)),
            pltpu.SemaphoreType.DMA((6,)),
        ],
        compiler_params=pltpu.CompilerParams(
            collective_id=0, has_side_effects=True, vmem_limit_bytes=60 << 20
        ),
        name="exchange_all",
    )(pivot, border, slots)


def load_rows(where_ref, pieces, raw):
    y = where_ref[2] // 2
    for d in range(RING):
        at = pl.multiple_of(((y + RING - d) % RING) * 2 * NB, 2 * NB)
        raw[:, pl.ds(at, 2 * NB)] = jnp.concatenate([pieces[d][0], pieces[d][1]], axis=1)
    return raw[...]


def rest_kernel(where_ref, *refs):
    pieces, (own_hi_ref, own_lo_ref, border_ref, raw) = refs[:RING], refs[RING:]
    raw_hi, raw_lo = split(load_rows(where_ref, pieces, raw))
    border_ref[...] = dot3_nt(raw_hi, raw_lo, own_hi_ref[0], own_lo_ref[0])


def solve_rest(where, pieces, inv_hi, inv_lo, tile=384):
    size = inv_hi.shape[2]
    rows = pieces[0].shape[1]
    own_spec = pl.BlockSpec((1, NB, size), lambda i, w: (0, w[2], 0))
    return pl.pallas_call(
        rest_kernel,
        grid_spec=pltpu.PrefetchScalarGridSpec(
            num_scalar_prefetch=1,
            grid=(rows // tile,),
            in_specs=[pl.BlockSpec((2, tile, NB), lambda i, w: (0, i, 0))] * RING + [own_spec] * 2,
            out_specs=pl.BlockSpec((tile, NB), lambda i, w: (i, 0)),
            scratch_shapes=[pltpu.VMEM((tile, size), F32)],
        ),
        out_shape=jax.ShapeDtypeStruct((rows, NB), F32),
        compiler_params=pltpu.CompilerParams(vmem_limit_bytes=60 << 20),
        name="solve_rest",
        cost_estimate=pl.CostEstimate(flops=600_000_000, bytes_accessed=4 << 20, transcendentals=0),
    )(where, *pieces, inv_hi, inv_lo)


def rows_kernel(where_ref, *refs):
    pieces, (inv_hi_ref, inv_lo_ref, own_hi_ref, own_lo_ref, hi_ref, lo_ref, border_ref, raw) = refs[:RING], refs[RING:]
    size = inv_hi_ref.shape[2]
    wide = 256
    raw_hi, raw_lo = split(load_rows(where_ref, pieces, raw))
    border_ref[...] = dot3_nt(raw_hi, raw_lo, own_hi_ref[0], own_lo_ref[0])
    solved = []
    for n in range(0, size, wide):
        part = slice(0, n + wide)
        at = slice(n, n + wide)
        solved.append(
            dot3_nt(raw_hi[:, part], raw_lo[:, part], inv_hi_ref[0, at, part], inv_lo_ref[0, at, part])
        )
    solved_hi, solved_lo = split(jnp.concatenate(solved, axis=1))
    for n in range(0, size, wide):
        at = slice(n, n + wide)
        out = dot3_nn(solved_hi[:, n:], solved_lo[:, n:], inv_hi_ref[0, n:, at], inv_lo_ref[0, n:, at])
        for q in range(2):
            k = n // NB + q
            into = slice((k // 2) * NB, (k // 2 + 1) * NB)
            hi_ref[k % 2, :, into], lo_ref[k % 2, :, into] = split(out[:, q * NB : (q + 1) * NB])


def solve_both(where, pieces, inv_hi, inv_lo, tile=320):
    fronts, size, _ = inv_hi.shape
    per = pieces[0].shape[1] // fronts
    tiles = per // tile
    inv_spec = pl.BlockSpec((1, size, size), lambda f, i, w: (f, 0, 0))
    own_spec = pl.BlockSpec((1, NB, size), lambda f, i, w: (f, w[2], 0))
    out_spec = pl.BlockSpec((2, tile, RING * NB), lambda f, i, w: (f, i, 0))
    return pl.pallas_call(
        rows_kernel,
        grid_spec=pltpu.PrefetchScalarGridSpec(
            num_scalar_prefetch=1,
            grid=(fronts, tiles),
            in_specs=[pl.BlockSpec((2, tile, NB), lambda f, i, w: (0, f * tiles + i, 0))] * RING
            + [inv_spec] * 2
            + [own_spec] * 2,
            out_specs=[out_spec] * 2 + [pl.BlockSpec((tile, NB), lambda f, i, w: (f * tiles + i, 0))],
            scratch_shapes=[pltpu.VMEM((tile, size), F32)],
        ),
        out_shape=[jax.ShapeDtypeStruct((2 * fronts, per, RING * NB), BF16)] * 2
        + [jax.ShapeDtypeStruct((fronts * per, NB), F32)],
        compiler_params=pltpu.CompilerParams(vmem_limit_bytes=60 << 20),
        name="solve_both",
        cost_estimate=pl.CostEstimate(flops=12_000_000_000, bytes_accessed=18 << 20, transcendentals=0),
    )(where, *pieces, inv_hi, inv_lo, inv_hi, inv_lo)


STEPS = (
    (1, 0), (3, 0), (0, 1), (0, 3),
    (1, 1), (3, 3), (1, 3), (3, 1),
    (1, 2), (3, 2), (2, 0),
    (2, 1), (2, 3), (0, 2), (2, 2),
)


def scatter_kernel(sent_ref, arrived_ref, send, recv, local):
    s, r, c = lax.axis_index("sub"), lax.axis_index("row"), lax.axis_index("col")
    per_front = sent_ref.shape[0] // 2
    group = s * per_front + r
    x, z = 2 * s + r % 2, r // 2
    others, where_to = [], []
    for dx, dz in STEPS:
        tx, tz = (x + dx) % RING, (z + dz) % RING
        to = {"sub": tx // 2, "row": 2 * tz + tx % 2, "col": c}
        where_to.append(to)
        others.append(to["sub"] * per_front + to["row"])
    barrier = pltpu.get_barrier_semaphore()
    for to in where_to:
        pl.semaphore_signal(barrier, inc=1, device_id=to, device_id_type=MESH)
    pl.semaphore_wait(barrier, len(where_to))
    copies = [
        pltpu.make_async_remote_copy(
            src_ref=sent_ref.at[g],
            dst_ref=arrived_ref.at[group],
            send_sem=send.at[n],
            recv_sem=recv.at[n],
            device_id=to,
            device_id_type=MESH,
        )
        for n, (g, to) in enumerate(zip(others, where_to))
    ]
    for item in copies:
        item.start()
    keep = pltpu.make_async_copy(sent_ref.at[group], arrived_ref.at[group], local)
    keep.start()
    keep.wait()
    for item in copies:
        item.wait_recv()
    for item in copies:
        item.wait_send()


def scatter_rows(sent):
    others = sent.shape[0] - 1
    return pl.pallas_call(
        scatter_kernel,
        in_specs=[pl.BlockSpec(memory_space=pl.ANY)],
        out_specs=pl.BlockSpec(memory_space=pl.ANY),
        out_shape=jax.ShapeDtypeStruct(sent.shape, F32),
        scratch_shapes=[
            pltpu.SemaphoreType.DMA((others,)),
            pltpu.SemaphoreType.DMA((others,)),
            pltpu.SemaphoreType.DMA,
        ],
        compiler_params=pltpu.CompilerParams(
            collective_id=1, has_side_effects=True, vmem_limit_bytes=60 << 20
        ),
        name="scatter_rows",
    )(sent)


def gather_rows(source, index_ref, base, width):
    sub = lax.broadcasted_iota(jnp.int32, (8, width), 0)
    picked = None
    for r in range(8):
        row = jnp.broadcast_to(source[pl.ds(index_ref[base + r], 1), :], (8, width))
        picked = row if picked is None else jnp.where(sub == r, row, picked)
    return picked


def product_kernel(where_ref, order_ref, *refs):
    split_z = len(refs[:-5]) == RING
    sides = refs[:-5]
    hi_ref, lo_ref, window_ref, out_ref, updated = refs[-5:]
    low, z = where_ref[1] % 2, where_ref[1] // 2

    def lanes(k):
        return pl.ds(pl.multiple_of(k * NB, NB), NB)

    total = None
    for at in range(2):
        if split_z:
            order = [(z + RING - d) % RING for d in range(RING)]
            c_hi, c_lo = split(jnp.concatenate([side[at] for side in sides], axis=1))
            t_hi = jnp.concatenate([hi_ref[at, :, lanes(k)] for k in order], axis=1)
            t_lo = jnp.concatenate([lo_ref[at, :, lanes(k)] for k in order], axis=1)
        else:
            own = (low + at) % 2
            c_hi, c_lo = split(jnp.concatenate([sides[at][k] for k in range(RING)], axis=1))
            t_hi, t_lo = hi_ref[own], lo_ref[own]
        part = dot3_nt(t_hi, t_lo, c_hi, c_lo)
        total = part if total is None else total + part
    updated[...] = window_ref[...] - total
    width = out_ref.shape[1]

    def group(s, carry):
        for q in range(2):
            base = pl.multiple_of(s * 16 + q * 8, 8)
            out_ref[pl.ds(base, 8), :] = gather_rows(updated, order_ref, base, width)
        return carry

    lax.fori_loop(0, out_ref.shape[0] // 16, group, 0)


def product(where, order, sides, rows_hi, rows_lo, window, first, tile=512):
    _, rows, _ = rows_hi.shape
    depth, tall, _ = sides[0].shape
    tiles = tall // tile
    rows_spec = pl.BlockSpec(rows_hi.shape, lambda i, w, o: (0, 0, 0), pipeline_mode=pl.Buffered(1))
    return pl.pallas_call(
        product_kernel,
        grid_spec=pltpu.PrefetchScalarGridSpec(
            num_scalar_prefetch=2,
            grid=(tiles,),
            in_specs=[pl.BlockSpec((depth, tile, NB), lambda i, w, o: (0, i, 0))] * len(sides)
            + [rows_spec] * 2
            + [pl.BlockSpec((rows, tile), lambda i, w, o: (0, first * tiles + i))],
            out_specs=pl.BlockSpec((rows, tile), lambda i, w, o: (0, i)),
            scratch_shapes=[pltpu.VMEM((rows, tile), F32)],
        ),
        out_shape=jax.ShapeDtypeStruct((rows, tall), F32),
        compiler_params=pltpu.CompilerParams(vmem_limit_bytes=60 << 20),
        name="product",
        cost_estimate=pl.CostEstimate(flops=9_000_000_000, bytes_accessed=20 << 20, transcendentals=0),
    )(where, order, *sides, rows_hi, rows_lo, window)


def assemble_kernel(first_ref, second_ref, arrived_ref, *refs):
    out_ref = refs[-1]
    per, width = out_ref.shape

    def group(s, carry):
        for q in range(2):
            base = pl.multiple_of(s * 16 + q * 8, 8)
            out_ref[pl.ds(base, 8), :] = gather_rows(arrived_ref, first_ref, base, width) + gather_rows(
                arrived_ref, second_ref, base, width
            )
        return carry

    lax.fori_loop(0, per // 16, group, 0)


def assemble(place, arrived, parent, first, width, tile=512):
    total, cols = arrived.shape
    per = place.shape[0] // 2
    tiles = cols // tile
    extra = [] if parent is None else [parent]
    return pl.pallas_call(
        assemble_kernel,
        grid_spec=pltpu.PrefetchScalarGridSpec(
            num_scalar_prefetch=2,
            grid=(tiles,),
            in_specs=[pl.BlockSpec((total, tile), lambda i, p, q: (0, i))]
            + [pl.BlockSpec(memory_space=pl.ANY)] * len(extra),
            out_specs=pl.BlockSpec((per, tile), lambda i, p, q: (0, first * tiles + i)),
        ),
        out_shape=jax.ShapeDtypeStruct((per, width), F32),
        input_output_aliases={3: 0} if extra else {},
        compiler_params=pltpu.CompilerParams(vmem_limit_bytes=60 << 20),
        name="assemble",
        cost_estimate=pl.CostEstimate(flops=4_000_000, bytes_accessed=8 << 20, transcendentals=0),
    )(place[:per], place[per:], arrived, *extra)


def per_device(pivot_panel, border_panel, window, assembly_map):
    front = lax.axis_index("sub")
    row_index = lax.axis_index("row")
    col_index = lax.axis_index("col")
    fronts, n_row, n_col = lax.axis_size("sub"), lax.axis_size("row"), lax.axis_size("col")
    pivot_local, border_local, window_local = pivot_panel[0], border_panel[0], window[0]
    size = n_row * pivot_local.shape[0]
    rows_kept, width = window_local.shape
    groups = fronts * n_row
    per = rows_kept // fronts
    capacity = rows_kept // groups
    both = ("sub", "row")
    where = jnp.stack([front, row_index, col_index])

    def exchange(x):
        return lax.all_to_all(x, both, split_axis=0, concat_axis=0, tiled=True)

    targets, ordering = lax.sort((assembly_map[0], lax.iota(jnp.int32, rows_kept)), num_keys=1)
    slots = jnp.pad((targets % per).reshape(groups, 1, capacity), ((0, 0), (0, 7), (0, NB - capacity)))
    pivots, half_a, half_b, rows, rest, slots = exchange_all(pivot_local, border_local, slots, rows_kept)

    beside = [(r, r ^ 1) for r in range(n_row)]
    side_a = [half_a, lax.ppermute(half_a, "row", beside)]
    side_b = [half_b]
    pieces, others = [rows], [rest]
    for d in (1, 2, 3):
        side_b.append(lax.ppermute(half_b, "row", [(r, (r + 2 * d) % n_row) for r in range(n_row)]))
        pieces.append(lax.ppermute(rows, "col", [(c, (c + 2 * d) % n_col) for c in range(n_col)]))
    for d in (1, 2, 3):
        others.append(lax.ppermute(rest, "col", [(c, (c + 2 * d) % n_col) for c in range(n_col)]))

    inv_hi, inv_lo, pivot_factor = factor_fronts(where, pivots, 1, size)

    owner = lax.iota(jnp.int32, rows_kept) // per
    _, place = lax.sort(
        (slots[:, 0, :capacity].reshape(-1) + owner * per, lax.iota(jnp.int32, rows_kept)), num_keys=1
    )

    rows_hi, rows_lo, border_kept = solve_both(where, pieces, inv_hi, inv_lo)
    side_a, side_b, others = lax.optimization_barrier((side_a, side_b, others))
    parent, arrived = None, []
    for first, sides in enumerate((side_a, side_b)):
        sent = product(where, ordering, sides, rows_hi, rows_lo, window_local, first)
        move = exchange if first == 0 else scatter_rows
        arrived.append(move(sent.reshape(groups, capacity, -1)).reshape(rows_kept, -1))
    border_factor = jnp.concatenate([border_kept, solve_rest(where, others, inv_hi, inv_lo)], axis=0)
    for first in range(2):
        parent = assemble(place, arrived[first], parent, first, width)
    return (pivot_factor[None], border_factor[None], parent)


def solution(mesh):
    in_specs = (
        P("sub", "row", "col"),
        P("sub", "row", "col"),
        P("sub", "row", "col"),
        P("sub", "row"),
    )
    out_specs = (P("sub", "row", "col"), P("sub", "row", "col"), P(("sub", "row"), "col"))
    return jax.shard_map(
        per_device, mesh=mesh, in_specs=in_specs, out_specs=out_specs, check_vma=False
    )
```

```python
import functools

import jax
import jax.numpy as jnp
from jax import lax
from jax.experimental import pallas as pl
from jax.experimental.pallas import tpu as pltpu
from jax.sharding import PartitionSpec as P

NB = 128
F32 = jnp.float32
BF16 = jnp.bfloat16


def split(x):
    hi = x.astype(BF16)
    return hi, (x - hi.astype(F32)).astype(BF16)


def dot_nn(a, b):
    return lax.dot_general(a, b, (((1,), (0,)), ((), ())), preferred_element_type=F32)


def dot_nt(a, b):
    return lax.dot_general(a, b, (((1,), (1,)), ((), ())), preferred_element_type=F32)


def dot3_nn(a_hi, a_lo, b_hi, b_lo):
    return dot_nn(jnp.concatenate([a_hi, a_lo, a_hi], axis=1), jnp.concatenate([b_hi, b_hi, b_lo], axis=0))


def dot3_nt(a_hi, a_lo, b_hi, b_lo):
    return dot_nt(jnp.concatenate([a_hi, a_lo, a_hi], axis=1), jnp.concatenate([b_hi, b_hi, b_lo], axis=1))


def eliminate(blocks):
    lane = lax.broadcasted_iota(jnp.int32, (8, NB), 1)
    sub = lax.broadcasted_iota(jnp.int32, (8, NB), 0)
    shape = (8, NB)
    for g in range(NB // 8):
        first = 8 * g
        for block in blocks:
            rows = [jnp.broadcast_to(block[g][k : k + 1, :], shape) for k in range(8)]
            scalar = {
                (k, n): jnp.broadcast_to(rows[k][:, first + n : first + n + 1], shape)
                for k in range(8)
                for n in range(k, 8)
            }
            inverse, factor = [], {}
            for k in range(8):
                inv = 1.0 / scalar[k, k]
                inverse.append(inv)
                unit = jnp.where(lane == first + k, 1.0, rows[k])
                for n in range(k + 1, 8):
                    m = scalar[k, n] * inv
                    factor[k, n] = m
                    for q in range(n, 8):
                        scalar[n, q] = scalar[n, q] - m * scalar[k, q]
                    rows[n] = jnp.where(lane == first + k, 0.0, rows[n]) - m * unit
            scaled = []
            for k in range(8):
                hat = jnp.where(lane == first + k, 1.0, rows[k])
                if k < 7:
                    hat = jnp.where(jnp.logical_and(lane > first + k, lane < first + 8), 0.0, hat)
                scaled.append(hat * inverse[k])
            for i in range(g + 1, NB // 8):
                column = [jnp.broadcast_to(block[i][:, first + k : first + k + 1], shape) for k in range(8)]
                for k in range(8):
                    for n in range(k + 1, 8):
                        column[n] = column[n] - column[k] * factor[k, n]
                inside = jnp.logical_and(lane >= first, lane < first + 8)
                rest = jnp.where(inside, 0.0, block[i])
                even = column[0] * scaled[0]
                odd = column[1] * scaled[1]
                for k in range(2, 8, 2):
                    even = even + column[k] * scaled[k]
                    odd = odd + column[k + 1] * scaled[k + 1]
                block[i] = rest - (even + odd)
            own = rows[0]
            for k in range(1, 8):
                own = jnp.where(sub == k, rows[k], own)
            block[g] = own
    return blocks


def factor_kernel(where_ref, pivot_ref, hi_ref, lo_ref, factor_ref, work, panel):
    fronts = work.shape[0]
    size = work.shape[1]
    steps = size // NB
    row_at, col_at = where_ref[1], where_ref[2]
    for f in range(fronts):
        for r in range(steps):
            for c in range(steps):
                work[f, r * NB : (r + 1) * NB, c * NB : (c + 1) * NB] = pivot_ref[c % 2, c // 2, r // 2, r % 2]
    lane = lax.broadcasted_iota(jnp.int32, (NB, NB), 1)
    sub = lax.broadcasted_iota(jnp.int32, (NB, NB), 0)
    factor_ref[...] = jnp.zeros_like(factor_ref)

    def step(j, carry):
        base = pl.multiple_of(j * NB, NB)
        here = pl.ds(base, NB)
        blocks = []
        for f in range(fronts):
            blocks.append([work[f, pl.ds(base + 8 * i, 8), here] for i in range(NB // 8)])
        blocks = eliminate(blocks)
        columns = lax.broadcasted_iota(jnp.int32, (NB, size), 1)
        rows = lax.broadcasted_iota(jnp.int32, (size, NB), 0)
        for f in range(fronts):
            done = jnp.concatenate(blocks[f], axis=0)
            diag = jnp.sum(jnp.where(lane == sub, done, 0.0), axis=1, keepdims=True)
            scale = lax.rsqrt(diag)
            inverse = jnp.where(lane < sub, done, jnp.where(lane == sub, 1.0, 0.0)) * scale
            upper = jnp.where(lane >= sub, done, 0.0) * scale
            inv_hi, inv_lo = split(inverse)
            below_hi, below_lo = split(work[f, :, here])
            left = dot3_nt(below_hi, below_lo, inv_hi, inv_lo)
            left = jnp.where(rows >= base + NB, left, 0.0)
            panel[f] = left
            work[f, here, here] = jnp.zeros((NB, NB), F32)
            right_hi, right_lo = split(work[f, here, :])
            right = dot3_nn(inv_hi, inv_lo, right_hi, right_lo)
            work[f, here, :] = right
            work[f, here, here] = inverse
            full = work[f, here, :]
            lower = jnp.where(columns < base + NB, full, 0.0)
            low_hi, low_lo = split(lower)
            hi_ref[f, here, :] = low_hi
            lo_ref[f, here, :] = low_lo
            full_hi, full_lo = split(full)
            stacked = jnp.concatenate([full_hi, full_hi, full_lo], axis=0)

            @pl.when(j == col_at)
            def _():
                factor_ref[...] = jnp.where(
                    row_at == j, upper.T, panel[f, pl.ds(pl.multiple_of(row_at * NB, NB), NB), :]
                )

            def trail(i, carry):
                at = pl.ds(pl.multiple_of(i * NB, NB), NB)
                work[f, at, here] = jnp.zeros((NB, NB), F32)
                l_hi, l_lo = split(panel[f, at, :])
                work[f, at, :] -= dot_nn(jnp.concatenate([l_hi, l_lo, l_hi], axis=1), stacked)
                return carry

            lax.fori_loop(j + 1, steps, trail, 0)
        return carry

    lax.fori_loop(0, steps, step, 0)


def factor_fronts(where, pivots, fronts, size):
    return pl.pallas_call(
        factor_kernel,
        in_specs=[pl.BlockSpec(memory_space=pltpu.SMEM), pl.BlockSpec(memory_space=pltpu.VMEM)],
        out_specs=[pl.BlockSpec(memory_space=pltpu.VMEM)] * 3,
        out_shape=[
            jax.ShapeDtypeStruct((fronts, size, size), BF16),
            jax.ShapeDtypeStruct((fronts, size, size), BF16),
            jax.ShapeDtypeStruct((NB, NB), F32),
        ],
        scratch_shapes=[pltpu.VMEM((fronts, size, size), F32), pltpu.VMEM((fronts, size, NB), F32)],
        compiler_params=pltpu.CompilerParams(vmem_limit_bytes=60 << 20),
        name="factor_fronts",
        cost_estimate=pl.CostEstimate(flops=20_000_000_000, bytes_accessed=16 << 20, transcendentals=0),
    )(where, pivots)


MESH = pl.DeviceIdType.MESH
RING = 4


def exchange_kernel(
    pivot_ref, border_ref, slots_ref, pivots, half_a, half_b, rows_out, rest_out, slots_out, send, recv, local
):
    s, r, c = lax.axis_index("sub"), lax.axis_index("row"), lax.axis_index("col")
    low, z, y, core = r % 2, r // 2, c // 2, c % 2

    def device(low, y, z, core):
        return {"sub": s, "row": 2 * z + low, "col": 2 * y + core}

    along_y = [device(low, (y + d) % RING, z, core) for d in (1, 2, 3)]
    along_z = [device(low, y, (z + d) % RING, core) for d in (1, 2, 3)]
    beside = device(1 - low, y, z, core)
    mate = device(low, y, z, 1 - core)
    turned = {"sub": s, "row": c, "col": r}
    groups = slots_ref.shape[0]
    per_front = groups // 2
    group = s * per_front + r
    plane = [(group + o) % groups for o in range(1, groups)]
    spread_to = [{"sub": g // per_front, "row": g % per_front, "col": c} for g in plane]
    count = [0]

    def copy(src, dst, to):
        n = count[0]
        count[0] += 1
        return pltpu.make_async_remote_copy(
            src_ref=src, dst_ref=dst, send_sem=send.at[n], recv_sem=recv.at[n], device_id=to, device_id_type=MESH
        )

    barrier = pltpu.get_barrier_semaphore()
    peers = along_y + [mate] + spread_to
    for peer in peers:
        pl.semaphore_signal(barrier, inc=1, device_id=peer, device_id_type=MESH)

    @pl.when(r != c)
    def _():
        pl.semaphore_signal(barrier, inc=1, device_id=turned, device_id_type=MESH)

    pl.semaphore_wait(barrier, len(peers) + (r != c).astype(jnp.int32))

    tall = half_a.shape[1]
    kept = rows_out.shape[1]
    rest = rest_out.shape[1]
    half = NB // 2
    one, two = pl.ds(0, half), pl.ds(half, half)

    first = [copy(pivot_ref.at[one], pivots.at[core, y, z, low, one], to) for to in along_z]
    first += [copy(pivot_ref.at[two], pivots.at[core, y, z, low, two], to) for to in along_y]
    for item in first:
        item.start()
    own = [
        pltpu.make_async_copy(pivot_ref, pivots.at[core, y, z, low], local.at[0]),
        pltpu.make_async_copy(border_ref.at[pl.ds(0, kept)], rows_out.at[core], local.at[1]),
        pltpu.make_async_copy(border_ref.at[pl.ds(kept, rest)], rest_out.at[core], local.at[5]),
    ]
    for item in own:
        item.start()
    swap_rows = copy(border_ref.at[pl.ds(0, kept)], rows_out.at[core], mate)
    swap_rest = copy(border_ref.at[pl.ds(kept, rest)], rest_out.at[core], mate)
    swap_rows.start()
    swap_rest.start()
    turn_a = copy(border_ref.at[pl.ds(0, tall)], half_a.at[c // 2], turned)
    turn_b = copy(border_ref.at[pl.ds(tall, tall)], half_b.at[c % 2], turned)
    keep_a = pltpu.make_async_copy(border_ref.at[pl.ds(0, tall)], half_a.at[z], local.at[2])
    keep_b = pltpu.make_async_copy(border_ref.at[pl.ds(tall, tall)], half_b.at[low], local.at[3])

    @pl.when(r != c)
    def _():
        turn_a.start()
        turn_b.start()

    @pl.when(r == c)
    def _():
        keep_a.start()
        keep_b.start()

    keep_slots = pltpu.make_async_copy(slots_ref.at[group], slots_out.at[group], local.at[4])
    keep_slots.start()
    spread = [copy(slots_ref.at[g], slots_out.at[group], to) for g, to in zip(plane, spread_to)]
    for item in spread:
        item.start()

    own[0].wait()
    for item in first:
        item.wait_recv()
    area_one, area_two = pivots.at[core, y, :, low, one], pivots.at[core, :, z, low, two]
    second = [copy(area_one, area_one, beside), copy(area_two, area_two, beside)]
    for item in second:
        item.start()

    for item in second:
        item.wait_recv()
    area_one, area_two = pivots.at[core, y, :, :, one], pivots.at[core, :, z, :, two]
    third = [copy(area_one, area_one, to) for to in along_y]
    third += [copy(area_two, area_two, to) for to in along_z]
    swaps = [copy(area_one, area_one, mate), copy(area_two, area_two, mate)]
    for item in third + swaps:
        item.start()

    @pl.when(r != c)
    def _():
        turn_a.wait_recv()
        turn_b.wait_recv()

    @pl.when(r == c)
    def _():
        keep_a.wait()
        keep_b.wait()

    stage = [copy(half_a.at[z], half_a.at[z], to) for to in along_z]
    stage += [copy(half_b.at[low], half_b.at[low], beside)]
    for item in stage:
        item.start()
    for d in (1, 2, 3):
        third[d - 1].wait_recv()
        area = pivots.at[core, (y + RING - d) % RING, :, :, one]
        swaps.append(copy(area, area, mate))
        swaps[-1].start()
        third[d + 2].wait_recv()
        area = pivots.at[core, :, (z + RING - d) % RING, :, two]
        swaps.append(copy(area, area, mate))
        swaps[-1].start()

    own[1].wait()
    own[2].wait()
    keep_slots.wait()
    for item in swaps + stage + spread + [swap_rows, swap_rest]:
        item.wait_recv()
    for item in first + second + third + swaps + stage + spread + [swap_rows, swap_rest]:
        item.wait_send()

    @pl.when(r != c)
    def _():
        turn_a.wait_send()
        turn_b.wait_send()


def exchange_all(pivot, border, slots, kept):
    tall = border.shape[0] // 2
    copies = 33 + slots.shape[0] - 1
    return pl.pallas_call(
        exchange_kernel,
        in_specs=[pl.BlockSpec(memory_space=pltpu.VMEM)] * 3,
        out_specs=[pl.BlockSpec(memory_space=pl.ANY)] * 6,
        out_shape=[
            jax.ShapeDtypeStruct((2, RING, RING, 2, NB, NB), F32),
            jax.ShapeDtypeStruct((RING, tall, NB), F32),
            jax.ShapeDtypeStruct((2, tall, NB), F32),
            jax.ShapeDtypeStruct((2, kept, NB), F32),
            jax.ShapeDtypeStruct((2, border.shape[0] - kept, NB), F32),
            jax.ShapeDtypeStruct(slots.shape, jnp.int32),
        ],
        scratch_shapes=[
            pltpu.SemaphoreType.DMA((copies,)),
            pltpu.SemaphoreType.DMA((copies,)),
            pltpu.SemaphoreType.DMA((6,)),
        ],
        compiler_params=pltpu.CompilerParams(
            collective_id=0, has_side_effects=True, vmem_limit_bytes=60 << 20
        ),
        name="exchange_all",
    )(pivot, border, slots)


def load_rows(where_ref, pieces, raw):
    y = where_ref[2] // 2
    for d in range(RING):
        at = pl.multiple_of(((y + RING - d) % RING) * 2 * NB, 2 * NB)
        raw[:, pl.ds(at, 2 * NB)] = jnp.concatenate([pieces[d][0], pieces[d][1]], axis=1)
    return raw[...]


def rest_kernel(where_ref, *refs):
    pieces, (own_hi_ref, own_lo_ref, border_ref, raw) = refs[:RING], refs[RING:]
    raw_hi, raw_lo = split(load_rows(where_ref, pieces, raw))
    border_ref[...] = dot3_nt(raw_hi, raw_lo, own_hi_ref[0], own_lo_ref[0])


def solve_rest(where, pieces, inv_hi, inv_lo, tile=384):
    size = inv_hi.shape[2]
    rows = pieces[0].shape[1]
    own_spec = pl.BlockSpec((1, NB, size), lambda i, w: (0, w[2], 0))
    return pl.pallas_call(
        rest_kernel,
        grid_spec=pltpu.PrefetchScalarGridSpec(
            num_scalar_prefetch=1,
            grid=(rows // tile,),
            in_specs=[pl.BlockSpec((2, tile, NB), lambda i, w: (0, i, 0))] * RING + [own_spec] * 2,
            out_specs=pl.BlockSpec((tile, NB), lambda i, w: (i, 0)),
            scratch_shapes=[pltpu.VMEM((tile, size), F32)],
        ),
        out_shape=jax.ShapeDtypeStruct((rows, NB), F32),
        compiler_params=pltpu.CompilerParams(vmem_limit_bytes=60 << 20),
        name="solve_rest",
        cost_estimate=pl.CostEstimate(flops=600_000_000, bytes_accessed=4 << 20, transcendentals=0),
    )(where, *pieces, inv_hi, inv_lo)


def rows_kernel(where_ref, *refs):
    pieces, (inv_hi_ref, inv_lo_ref, own_hi_ref, own_lo_ref, hi_ref, lo_ref, border_ref, raw) = refs[:RING], refs[RING:]
    size = inv_hi_ref.shape[2]
    wide = 256
    raw_hi, raw_lo = split(load_rows(where_ref, pieces, raw))
    border_ref[...] = dot3_nt(raw_hi, raw_lo, own_hi_ref[0], own_lo_ref[0])
    solved = []
    for n in range(0, size, wide):
        part = slice(0, n + wide)
        at = slice(n, n + wide)
        solved.append(
            dot3_nt(raw_hi[:, part], raw_lo[:, part], inv_hi_ref[0, at, part], inv_lo_ref[0, at, part])
        )
    solved_hi, solved_lo = split(jnp.concatenate(solved, axis=1))
    for n in range(0, size, wide):
        at = slice(n, n + wide)
        out = dot3_nn(solved_hi[:, n:], solved_lo[:, n:], inv_hi_ref[0, n:, at], inv_lo_ref[0, n:, at])
        for q in range(2):
            k = n // NB + q
            into = slice((k // 2) * NB, (k // 2 + 1) * NB)
            hi_ref[k % 2, :, into], lo_ref[k % 2, :, into] = split(out[:, q * NB : (q + 1) * NB])


def solve_both(where, pieces, inv_hi, inv_lo, tile=320):
    fronts, size, _ = inv_hi.shape
    per = pieces[0].shape[1] // fronts
    tiles = per // tile
    inv_spec = pl.BlockSpec((1, size, size), lambda f, i, w: (f, 0, 0))
    own_spec = pl.BlockSpec((1, NB, size), lambda f, i, w: (f, w[2], 0))
    out_spec = pl.BlockSpec((2, tile, RING * NB), lambda f, i, w: (f, i, 0))
    return pl.pallas_call(
        rows_kernel,
        grid_spec=pltpu.PrefetchScalarGridSpec(
            num_scalar_prefetch=1,
            grid=(fronts, tiles),
            in_specs=[pl.BlockSpec((2, tile, NB), lambda f, i, w: (0, f * tiles + i, 0))] * RING
            + [inv_spec] * 2
            + [own_spec] * 2,
            out_specs=[out_spec] * 2 + [pl.BlockSpec((tile, NB), lambda f, i, w: (f * tiles + i, 0))],
            scratch_shapes=[pltpu.VMEM((tile, size), F32)],
        ),
        out_shape=[jax.ShapeDtypeStruct((2 * fronts, per, RING * NB), BF16)] * 2
        + [jax.ShapeDtypeStruct((fronts * per, NB), F32)],
        compiler_params=pltpu.CompilerParams(vmem_limit_bytes=60 << 20),
        name="solve_both",
        cost_estimate=pl.CostEstimate(flops=12_000_000_000, bytes_accessed=18 << 20, transcendentals=0),
    )(where, *pieces, inv_hi, inv_lo, inv_hi, inv_lo)


STEPS = (
    (1, 0), (3, 0), (0, 1), (0, 3),
    (1, 1), (3, 3), (1, 3), (3, 1),
    (1, 2), (3, 2), (2, 0),
    (2, 1), (2, 3), (0, 2), (2, 2),
)


def scatter_kernel(sent_ref, arrived_ref, send, recv, local):
    s, r, c = lax.axis_index("sub"), lax.axis_index("row"), lax.axis_index("col")
    per_front = sent_ref.shape[0] // 2
    group = s * per_front + r
    x, z = 2 * s + r % 2, r // 2
    others, where_to = [], []
    for dx, dz in STEPS:
        tx, tz = (x + dx) % RING, (z + dz) % RING
        to = {"sub": tx // 2, "row": 2 * tz + tx % 2, "col": c}
        where_to.append(to)
        others.append(to["sub"] * per_front + to["row"])
    barrier = pltpu.get_barrier_semaphore()
    for to in where_to:
        pl.semaphore_signal(barrier, inc=1, device_id=to, device_id_type=MESH)
    pl.semaphore_wait(barrier, len(where_to))
    copies = [
        pltpu.make_async_remote_copy(
            src_ref=sent_ref.at[g],
            dst_ref=arrived_ref.at[group],
            send_sem=send.at[n],
            recv_sem=recv.at[n],
            device_id=to,
            device_id_type=MESH,
        )
        for n, (g, to) in enumerate(zip(others, where_to))
    ]
    for item in copies:
        item.start()
    keep = pltpu.make_async_copy(sent_ref.at[group], arrived_ref.at[group], local)
    keep.start()
    keep.wait()
    for item in copies:
        item.wait_recv()
    for item in copies:
        item.wait_send()


def scatter_rows(sent):
    others = sent.shape[0] - 1
    return pl.pallas_call(
        scatter_kernel,
        in_specs=[pl.BlockSpec(memory_space=pl.ANY)],
        out_specs=pl.BlockSpec(memory_space=pl.ANY),
        out_shape=jax.ShapeDtypeStruct(sent.shape, F32),
        scratch_shapes=[
            pltpu.SemaphoreType.DMA((others,)),
            pltpu.SemaphoreType.DMA((others,)),
            pltpu.SemaphoreType.DMA,
        ],
        compiler_params=pltpu.CompilerParams(
            collective_id=1, has_side_effects=True, vmem_limit_bytes=60 << 20
        ),
        name="scatter_rows",
    )(sent)


def gather_rows(source, index_ref, base, width):
    sub = lax.broadcasted_iota(jnp.int32, (8, width), 0)
    picked = None
    for r in range(8):
        row = jnp.broadcast_to(source[pl.ds(index_ref[base + r], 1), :], (8, width))
        picked = row if picked is None else jnp.where(sub == r, row, picked)
    return picked


def product_kernel(where_ref, order_ref, *refs):
    split_z = len(refs[:-5]) == RING
    sides = refs[:-5]
    hi_ref, lo_ref, window_ref, out_ref, updated = refs[-5:]
    low, z = where_ref[1] % 2, where_ref[1] // 2

    def lanes(k):
        return pl.ds(pl.multiple_of(k * NB, NB), NB)

    total = None
    for at in range(2):
        if split_z:
            order = [(z + RING - d) % RING for d in range(RING)]
            c_hi, c_lo = split(jnp.concatenate([side[at] for side in sides], axis=1))
            t_hi = jnp.concatenate([hi_ref[at, :, lanes(k)] for k in order], axis=1)
            t_lo = jnp.concatenate([lo_ref[at, :, lanes(k)] for k in order], axis=1)
        else:
            own = (low + at) % 2
            c_hi, c_lo = split(jnp.concatenate([sides[at][k] for k in range(RING)], axis=1))
            t_hi, t_lo = hi_ref[own], lo_ref[own]
        part = dot3_nt(t_hi, t_lo, c_hi, c_lo)
        total = part if total is None else total + part
    updated[...] = window_ref[...] - total
    width = out_ref.shape[1]

    def group(s, carry):
        for q in range(2):
            base = pl.multiple_of(s * 16 + q * 8, 8)
            out_ref[pl.ds(base, 8), :] = gather_rows(updated, order_ref, base, width)
        return carry

    lax.fori_loop(0, out_ref.shape[0] // 16, group, 0)


def product(where, order, sides, rows_hi, rows_lo, window, first, tile=512):
    _, rows, _ = rows_hi.shape
    depth, tall, _ = sides[0].shape
    tiles = tall // tile
    rows_spec = pl.BlockSpec(rows_hi.shape, lambda i, w, o: (0, 0, 0), pipeline_mode=pl.Buffered(1))
    return pl.pallas_call(
        product_kernel,
        grid_spec=pltpu.PrefetchScalarGridSpec(
            num_scalar_prefetch=2,
            grid=(tiles,),
            in_specs=[pl.BlockSpec((depth, tile, NB), lambda i, w, o: (0, i, 0))] * len(sides)
            + [rows_spec] * 2
            + [pl.BlockSpec((rows, tile), lambda i, w, o: (0, first * tiles + i))],
            out_specs=pl.BlockSpec((rows, tile), lambda i, w, o: (0, i)),
            scratch_shapes=[pltpu.VMEM((rows, tile), F32)],
        ),
        out_shape=jax.ShapeDtypeStruct((rows, tall), F32),
        compiler_params=pltpu.CompilerParams(vmem_limit_bytes=60 << 20),
        name="product",
        cost_estimate=pl.CostEstimate(flops=9_000_000_000, bytes_accessed=20 << 20, transcendentals=0),
    )(where, order, *sides, rows_hi, rows_lo, window)


def assemble_kernel(first_ref, second_ref, arrived_ref, *refs):
    out_ref = refs[-1]
    per, width = out_ref.shape

    def group(s, carry):
        for q in range(2):
            base = pl.multiple_of(s * 16 + q * 8, 8)
            out_ref[pl.ds(base, 8), :] = gather_rows(arrived_ref, first_ref, base, width) + gather_rows(
                arrived_ref, second_ref, base, width
            )
        return carry

    lax.fori_loop(0, per // 16, group, 0)


def assemble(place, arrived, parent, first, width, tile=512):
    total, cols = arrived.shape
    per = place.shape[0] // 2
    tiles = cols // tile
    extra = [] if parent is None else [parent]
    return pl.pallas_call(
        assemble_kernel,
        grid_spec=pltpu.PrefetchScalarGridSpec(
            num_scalar_prefetch=2,
            grid=(tiles,),
            in_specs=[pl.BlockSpec((total, tile), lambda i, p, q: (0, i))]
            + [pl.BlockSpec(memory_space=pl.ANY)] * len(extra),
            out_specs=pl.BlockSpec((per, tile), lambda i, p, q: (0, first * tiles + i)),
        ),
        out_shape=jax.ShapeDtypeStruct((per, width), F32),
        input_output_aliases={3: 0} if extra else {},
        compiler_params=pltpu.CompilerParams(vmem_limit_bytes=60 << 20),
        name="assemble",
        cost_estimate=pl.CostEstimate(flops=4_000_000, bytes_accessed=8 << 20, transcendentals=0),
    )(place[:per], place[per:], arrived, *extra)


def per_device(pivot_panel, border_panel, window, assembly_map):
    front = lax.axis_index("sub")
    row_index = lax.axis_index("row")
    col_index = lax.axis_index("col")
    fronts, n_row, n_col = lax.axis_size("sub"), lax.axis_size("row"), lax.axis_size("col")
    pivot_local, border_local, window_local = pivot_panel[0], border_panel[0], window[0]
    size = n_row * pivot_local.shape[0]
    rows_kept, width = window_local.shape
    groups = fronts * n_row
    per = rows_kept // fronts
    capacity = rows_kept // groups
    both = ("sub", "row")
    where = jnp.stack([front, row_index, col_index])

    def exchange(x):
        return lax.all_to_all(x, both, split_axis=0, concat_axis=0, tiled=True)

    targets, ordering = lax.sort((assembly_map[0], lax.iota(jnp.int32, rows_kept)), num_keys=1)
    slots = jnp.pad((targets % per).reshape(groups, 1, capacity), ((0, 0), (0, 7), (0, NB - capacity)))
    pivots, half_a, half_b, rows, rest, slots = exchange_all(pivot_local, border_local, slots, rows_kept)

    beside = [(r, r ^ 1) for r in range(n_row)]
    side_a = [half_a, lax.ppermute(half_a, "row", beside)]
    side_b = [half_b]
    pieces = [rows]
    for d in (1, 2, 3):
        side_b.append(lax.ppermute(half_b, "row", [(r, (r + 2 * d) % n_row) for r in range(n_row)]))
        pieces.append(lax.ppermute(rows, "col", [(c, (c + 2 * d) % n_col) for c in range(n_col)]))
    inv_hi, inv_lo, pivot_factor = factor_fronts(where, pivots, 1, size)
    rest, inv_hi, inv_lo = lax.optimization_barrier((rest, inv_hi, inv_lo))
    others = [rest]
    for d in (1, 2, 3):
        others.append(lax.ppermute(rest, "col", [(c, (c + 2 * d) % n_col) for c in range(n_col)]))

    owner = lax.iota(jnp.int32, rows_kept) // per
    _, place = lax.sort(
        (slots[:, 0, :capacity].reshape(-1) + owner * per, lax.iota(jnp.int32, rows_kept)), num_keys=1
    )

    rows_hi, rows_lo, border_kept = solve_both(where, pieces, inv_hi, inv_lo)
    side_a, side_b = lax.optimization_barrier((side_a, side_b))
    parent, arrived = None, []
    for first, sides in enumerate((side_a, side_b)):
        sent = product(where, ordering, sides, rows_hi, rows_lo, window_local, first)
        if first == 1:
            others, sent = lax.optimization_barrier((others, sent))
            border_rest = solve_rest(where, others, inv_hi, inv_lo)
            sent, border_rest = lax.optimization_barrier((sent, border_rest))
        move = exchange if first == 0 else scatter_rows
        arrived.append(move(sent.reshape(groups, capacity, -1)).reshape(rows_kept, -1))
    border_factor = jnp.concatenate([border_kept, border_rest], axis=0)
    for first in range(2):
        parent = assemble(place, arrived[first], parent, first, width)
    return (pivot_factor[None], border_factor[None], parent)


def solution(mesh):
    in_specs = (
        P("sub", "row", "col"),
        P("sub", "row", "col"),
        P("sub", "row", "col"),
        P("sub", "row"),
    )
    out_specs = (P("sub", "row", "col"), P("sub", "row", "col"), P(("sub", "row"), "col"))
    return jax.shard_map(
        per_device, mesh=mesh, in_specs=in_specs, out_specs=out_specs, check_vma=False
    )
```

```python
import functools

import jax
import jax.numpy as jnp
from jax import lax
from jax.experimental import pallas as pl
from jax.experimental.pallas import tpu as pltpu
from jax.sharding import PartitionSpec as P

NB = 128
F32 = jnp.float32
BF16 = jnp.bfloat16


def split(x):
    hi = x.astype(BF16)
    return hi, (x - hi.astype(F32)).astype(BF16)


def dot_nn(a, b):
    return lax.dot_general(a, b, (((1,), (0,)), ((), ())), preferred_element_type=F32)


def dot_nt(a, b):
    return lax.dot_general(a, b, (((1,), (1,)), ((), ())), preferred_element_type=F32)


def dot3_nn(a_hi, a_lo, b_hi, b_lo):
    return dot_nn(jnp.concatenate([a_hi, a_lo, a_hi], axis=1), jnp.concatenate([b_hi, b_hi, b_lo], axis=0))


def dot3_nt(a_hi, a_lo, b_hi, b_lo):
    return dot_nt(jnp.concatenate([a_hi, a_lo, a_hi], axis=1), jnp.concatenate([b_hi, b_hi, b_lo], axis=1))


def eliminate(blocks):
    lane = lax.broadcasted_iota(jnp.int32, (8, NB), 1)
    sub = lax.broadcasted_iota(jnp.int32, (8, NB), 0)
    shape = (8, NB)
    for g in range(NB // 8):
        first = 8 * g
        for block in blocks:
            rows = [jnp.broadcast_to(block[g][k : k + 1, :], shape) for k in range(8)]
            scalar = {
                (k, n): jnp.broadcast_to(rows[k][:, first + n : first + n + 1], shape)
                for k in range(8)
                for n in range(k, 8)
            }
            inverse, factor = [], {}
            for k in range(8):
                inv = 1.0 / scalar[k, k]
                inverse.append(inv)
                unit = jnp.where(lane == first + k, 1.0, rows[k])
                for n in range(k + 1, 8):
                    m = scalar[k, n] * inv
                    factor[k, n] = m
                    for q in range(n, 8):
                        scalar[n, q] = scalar[n, q] - m * scalar[k, q]
                    rows[n] = jnp.where(lane == first + k, 0.0, rows[n]) - m * unit
            scaled = []
            for k in range(8):
                hat = jnp.where(lane == first + k, 1.0, rows[k])
                if k < 7:
                    hat = jnp.where(jnp.logical_and(lane > first + k, lane < first + 8), 0.0, hat)
                scaled.append(hat * inverse[k])
            for i in range(g + 1, NB // 8):
                column = [jnp.broadcast_to(block[i][:, first + k : first + k + 1], shape) for k in range(8)]
                for k in range(8):
                    for n in range(k + 1, 8):
                        column[n] = column[n] - column[k] * factor[k, n]
                inside = jnp.logical_and(lane >= first, lane < first + 8)
                rest = jnp.where(inside, 0.0, block[i])
                even = column[0] * scaled[0]
                odd = column[1] * scaled[1]
                for k in range(2, 8, 2):
                    even = even + column[k] * scaled[k]
                    odd = odd + column[k + 1] * scaled[k + 1]
                block[i] = rest - (even + odd)
            own = rows[0]
            for k in range(1, 8):
                own = jnp.where(sub == k, rows[k], own)
            block[g] = own
    return blocks


def factor_steps(row_at, col_at, pivot_ref, hi_ref, lo_ref, factor_ref, work, panel, between):
    fronts = work.shape[0]
    size = work.shape[1]
    steps = size // NB
    for f in range(fronts):
        for r in range(steps):
            for c in range(steps):
                work[f, r * NB : (r + 1) * NB, c * NB : (c + 1) * NB] = pivot_ref[c % 2, c // 2, r // 2, r % 2]
    lane = lax.broadcasted_iota(jnp.int32, (NB, NB), 1)
    sub = lax.broadcasted_iota(jnp.int32, (NB, NB), 0)
    factor_ref[...] = jnp.zeros_like(factor_ref)

    def step(j, carry):
        between(j)
        base = pl.multiple_of(j * NB, NB)
        here = pl.ds(base, NB)
        blocks = []
        for f in range(fronts):
            blocks.append([work[f, pl.ds(base + 8 * i, 8), here] for i in range(NB // 8)])
        blocks = eliminate(blocks)
        columns = lax.broadcasted_iota(jnp.int32, (NB, size), 1)
        rows = lax.broadcasted_iota(jnp.int32, (size, NB), 0)
        for f in range(fronts):
            done = jnp.concatenate(blocks[f], axis=0)
            diag = jnp.sum(jnp.where(lane == sub, done, 0.0), axis=1, keepdims=True)
            scale = lax.rsqrt(diag)
            inverse = jnp.where(lane < sub, done, jnp.where(lane == sub, 1.0, 0.0)) * scale
            upper = jnp.where(lane >= sub, done, 0.0) * scale
            inv_hi, inv_lo = split(inverse)
            below_hi, below_lo = split(work[f, :, here])
            left = dot3_nt(below_hi, below_lo, inv_hi, inv_lo)
            left = jnp.where(rows >= base + NB, left, 0.0)
            panel[f] = left
            work[f, here, here] = jnp.zeros((NB, NB), F32)
            right_hi, right_lo = split(work[f, here, :])
            right = dot3_nn(inv_hi, inv_lo, right_hi, right_lo)
            work[f, here, :] = right
            work[f, here, here] = inverse
            full = work[f, here, :]
            lower = jnp.where(columns < base + NB, full, 0.0)
            low_hi, low_lo = split(lower)
            hi_ref[f, here, :] = low_hi
            lo_ref[f, here, :] = low_lo
            full_hi, full_lo = split(full)
            stacked = jnp.concatenate([full_hi, full_hi, full_lo], axis=0)

            @pl.when(j == col_at)
            def _():
                factor_ref[...] = jnp.where(
                    row_at == j, upper.T, panel[f, pl.ds(pl.multiple_of(row_at * NB, NB), NB), :]
                )

            def trail(i, carry):
                at = pl.ds(pl.multiple_of(i * NB, NB), NB)
                work[f, at, here] = jnp.zeros((NB, NB), F32)
                l_hi, l_lo = split(panel[f, at, :])
                work[f, at, :] -= dot_nn(jnp.concatenate([l_hi, l_lo, l_hi], axis=1), stacked)
                return carry

            lax.fori_loop(j + 1, steps, trail, 0)
        return carry

    lax.fori_loop(0, steps, step, 0)


MESH = pl.DeviceIdType.MESH
RING = 4


def exchange_kernel(
    pivot_ref, border_ref, slots_ref,
    side_a, side_b, rows_all, rest_out, slots_out, hi_ref, lo_ref, factor_ref,
    pivots, work, panel, send, recv, local,
):
    s, r, c = lax.axis_index("sub"), lax.axis_index("row"), lax.axis_index("col")
    low, z, y, core = r % 2, r // 2, c // 2, c % 2

    def device(low, y, z, core):
        return {"sub": s, "row": 2 * z + low, "col": 2 * y + core}

    along_y = [device(low, (y + d) % RING, z, core) for d in (1, 2, 3)]
    along_z = [device(low, y, (z + d) % RING, core) for d in (1, 2, 3)]
    beside = device(1 - low, y, z, core)
    mate = device(low, y, z, 1 - core)
    turned = {"sub": s, "row": c, "col": r}
    groups = slots_ref.shape[0]
    per_front = groups // 2
    group = s * per_front + r
    plane = [(group + o) % groups for o in range(1, groups)]
    spread_to = [{"sub": g // per_front, "row": g % per_front, "col": c} for g in plane]
    count = [0]

    def copy(src, dst, to):
        n = count[0]
        count[0] += 1
        return pltpu.make_async_remote_copy(
            src_ref=src, dst_ref=dst, send_sem=send.at[n], recv_sem=recv.at[n], device_id=to, device_id_type=MESH
        )

    barrier = pltpu.get_barrier_semaphore()
    peers = along_y + [mate] + spread_to
    for peer in peers:
        pl.semaphore_signal(barrier, inc=1, device_id=peer, device_id_type=MESH)

    @pl.when(r != c)
    def _():
        pl.semaphore_signal(barrier, inc=1, device_id=turned, device_id_type=MESH)

    pl.semaphore_wait(barrier, len(peers) + (r != c).astype(jnp.int32))

    tall = side_a.shape[2]
    kept = rows_all.shape[2]
    half_a, half_b, rows_out = side_a.at[low], side_b.at[z], rows_all.at[y]
    rest = rest_out.shape[1]
    half = NB // 2
    one, two = pl.ds(0, half), pl.ds(half, half)

    first = [copy(pivot_ref.at[one], pivots.at[core, y, z, low, one], to) for to in along_z]
    first += [copy(pivot_ref.at[two], pivots.at[core, y, z, low, two], to) for to in along_y]
    for item in first:
        item.start()
    own = [
        pltpu.make_async_copy(pivot_ref, pivots.at[core, y, z, low], local.at[0]),
        pltpu.make_async_copy(border_ref.at[pl.ds(0, kept)], rows_out.at[core], local.at[1]),
        pltpu.make_async_copy(border_ref.at[pl.ds(kept, rest)], rest_out.at[core], local.at[5]),
    ]
    for item in own:
        item.start()
    swap_rows = copy(border_ref.at[pl.ds(0, kept)], rows_out.at[core], mate)
    swap_rest = copy(border_ref.at[pl.ds(kept, rest)], rest_out.at[core], mate)
    swap_rows.start()
    swap_rest.start()
    turn_a = copy(border_ref.at[pl.ds(0, tall)], side_a.at[c % 2, c // 2], turned)
    turn_b = copy(border_ref.at[pl.ds(tall, tall)], side_b.at[c // 2, c % 2], turned)
    keep_a = pltpu.make_async_copy(border_ref.at[pl.ds(0, tall)], half_a.at[z], local.at[2])
    keep_b = pltpu.make_async_copy(border_ref.at[pl.ds(tall, tall)], half_b.at[low], local.at[3])

    @pl.when(r != c)
    def _():
        turn_a.start()
        turn_b.start()

    @pl.when(r == c)
    def _():
        keep_a.start()
        keep_b.start()

    keep_slots = pltpu.make_async_copy(slots_ref.at[group], slots_out.at[group], local.at[4])
    keep_slots.start()
    spread = [copy(slots_ref.at[g], slots_out.at[group], to) for g, to in zip(plane, spread_to)]
    for item in spread:
        item.start()

    own[0].wait()
    for item in first:
        item.wait_recv()
    area_one, area_two = pivots.at[core, y, :, low, one], pivots.at[core, :, z, low, two]
    second = [copy(area_one, area_one, beside), copy(area_two, area_two, beside)]
    for item in second:
        item.start()

    for item in second:
        item.wait_recv()
    area_one, area_two = pivots.at[core, y, :, :, one], pivots.at[core, :, z, :, two]
    third = [copy(area_one, area_one, to) for to in along_y]
    third += [copy(area_two, area_two, to) for to in along_z]
    swaps = [copy(area_one, area_one, mate), copy(area_two, area_two, mate)]
    for item in third + swaps:
        item.start()
    own[1].wait()
    swap_rows.wait_recv()
    spread_rows = [copy(rows_out, rows_out, to) for to in along_y]
    for item in spread_rows:
        item.start()

    @pl.when(r != c)
    def _():
        turn_a.wait_recv()
        turn_b.wait_recv()

    @pl.when(r == c)
    def _():
        keep_a.wait()
        keep_b.wait()

    stage = [copy(half_a.at[z], half_a.at[z], to) for to in along_z]
    stage += [copy(half_b.at[low], half_b.at[low], beside)]
    for item in stage:
        item.start()
    for d in (1, 2, 3):
        third[d - 1].wait_recv()
        area = pivots.at[core, (y + RING - d) % RING, :, :, one]
        swaps.append(copy(area, area, mate))
        swaps[-1].start()
        third[d + 2].wait_recv()
        area = pivots.at[core, :, (z + RING - d) % RING, :, two]
        swaps.append(copy(area, area, mate))
        swaps[-1].start()

    for item in swaps:
        item.wait_recv()
    last = [copy(half_a, half_a, beside)] + [copy(half_b, half_b, to) for to in along_z]

    def between(j):
        @pl.when(j == 1)
        def _():
            for item in stage:
                item.wait_recv()
            for item in last:
                item.start()

    factor_steps(r, c, pivots, hi_ref, lo_ref, factor_ref, work, panel, between)

    own[2].wait()
    keep_slots.wait()
    for item in spread_rows + last + spread + [swap_rest]:
        item.wait_recv()
    for item in first + second + third + swaps + stage + spread + spread_rows + last + [swap_rows, swap_rest]:
        item.wait_send()

    @pl.when(r != c)
    def _():
        turn_a.wait_send()
        turn_b.wait_send()


def exchange_all(pivot, border, slots, kept, size):
    tall = border.shape[0] // 2
    copies = 40 + slots.shape[0] - 1
    moved = pl.BlockSpec(memory_space=pl.ANY)
    near = pl.BlockSpec(memory_space=pltpu.VMEM)
    return pl.pallas_call(
        exchange_kernel,
        in_specs=[near] * 3,
        out_specs=[moved] * 5 + [near] * 3,
        out_shape=[
            jax.ShapeDtypeStruct((2, RING, tall, NB), F32),
            jax.ShapeDtypeStruct((RING, 2, tall, NB), F32),
            jax.ShapeDtypeStruct((RING, 2, kept, NB), F32),
            jax.ShapeDtypeStruct((2, border.shape[0] - kept, NB), F32),
            jax.ShapeDtypeStruct(slots.shape, jnp.int32),
            jax.ShapeDtypeStruct((1, size, size), BF16),
            jax.ShapeDtypeStruct((1, size, size), BF16),
            jax.ShapeDtypeStruct((NB, NB), F32),
        ],
        scratch_shapes=[
            pltpu.VMEM((2, RING, RING, 2, NB, NB), F32),
            pltpu.VMEM((1, size, size), F32),
            pltpu.VMEM((1, size, NB), F32),
            pltpu.SemaphoreType.DMA((copies,)),
            pltpu.SemaphoreType.DMA((copies,)),
            pltpu.SemaphoreType.DMA((6,)),
        ],
        compiler_params=pltpu.CompilerParams(
            collective_id=0, has_side_effects=True, vmem_limit_bytes=60 << 20
        ),
        name="exchange_all",
    )(pivot, border, slots)


def load_rows(where_ref, pieces, raw):
    y = where_ref[2] // 2
    for d in range(RING):
        at = pl.multiple_of(((y + RING - d) % RING) * 2 * NB, 2 * NB)
        raw[:, pl.ds(at, 2 * NB)] = jnp.concatenate([pieces[d][0], pieces[d][1]], axis=1)
    return raw[...]


def rest_kernel(where_ref, *refs):
    pieces, (own_hi_ref, own_lo_ref, border_ref, raw) = refs[:RING], refs[RING:]
    raw_hi, raw_lo = split(load_rows(where_ref, pieces, raw))
    border_ref[...] = dot3_nt(raw_hi, raw_lo, own_hi_ref[0], own_lo_ref[0])


def solve_rest(where, pieces, inv_hi, inv_lo, tile=384):
    size = inv_hi.shape[2]
    rows = pieces[0].shape[1]
    own_spec = pl.BlockSpec((1, NB, size), lambda i, w: (0, w[2], 0))
    return pl.pallas_call(
        rest_kernel,
        grid_spec=pltpu.PrefetchScalarGridSpec(
            num_scalar_prefetch=1,
            grid=(rows // tile,),
            in_specs=[pl.BlockSpec((2, tile, NB), lambda i, w: (0, i, 0))] * RING + [own_spec] * 2,
            out_specs=pl.BlockSpec((tile, NB), lambda i, w: (i, 0)),
            scratch_shapes=[pltpu.VMEM((tile, size), F32)],
        ),
        out_shape=jax.ShapeDtypeStruct((rows, NB), F32),
        compiler_params=pltpu.CompilerParams(vmem_limit_bytes=60 << 20),
        name="solve_rest",
        cost_estimate=pl.CostEstimate(flops=600_000_000, bytes_accessed=4 << 20, transcendentals=0),
    )(where, *pieces, inv_hi, inv_lo)


def rows_kernel(where_ref, *refs):
    rows_ref, inv_hi_ref, inv_lo_ref, own_hi_ref, own_lo_ref, hi_ref, lo_ref, border_ref = refs
    size = inv_hi_ref.shape[2]
    wide = 256
    raw_hi, raw_lo = split(jnp.concatenate([rows_ref[y, k] for y in range(RING) for k in range(2)], axis=1))
    border_ref[...] = dot3_nt(raw_hi, raw_lo, own_hi_ref[0], own_lo_ref[0])
    solved = []
    for n in range(0, size, wide):
        part = slice(0, n + wide)
        at = slice(n, n + wide)
        solved.append(
            dot3_nt(raw_hi[:, part], raw_lo[:, part], inv_hi_ref[0, at, part], inv_lo_ref[0, at, part])
        )
    solved_hi, solved_lo = split(jnp.concatenate(solved, axis=1))
    for n in range(0, size, wide):
        at = slice(n, n + wide)
        out = dot3_nn(solved_hi[:, n:], solved_lo[:, n:], inv_hi_ref[0, n:, at], inv_lo_ref[0, n:, at])
        for q in range(2):
            k = n // NB + q
            into = slice((k // 2) * NB, (k // 2 + 1) * NB)
            hi_ref[k % 2, :, into], lo_ref[k % 2, :, into] = split(out[:, q * NB : (q + 1) * NB])


def solve_both(where, rows, inv_hi, inv_lo, tile=320):
    fronts, size, _ = inv_hi.shape
    per = rows.shape[2] // fronts
    tiles = per // tile
    inv_spec = pl.BlockSpec((1, size, size), lambda f, i, w: (f, 0, 0))
    own_spec = pl.BlockSpec((1, NB, size), lambda f, i, w: (f, w[2], 0))
    out_spec = pl.BlockSpec((2, tile, RING * NB), lambda f, i, w: (f, i, 0))
    return pl.pallas_call(
        rows_kernel,
        grid_spec=pltpu.PrefetchScalarGridSpec(
            num_scalar_prefetch=1,
            grid=(fronts, tiles),
            in_specs=[pl.BlockSpec((RING, 2, tile, NB), lambda f, i, w: (0, 0, f * tiles + i, 0))]
            + [inv_spec] * 2
            + [own_spec] * 2,
            out_specs=[out_spec] * 2 + [pl.BlockSpec((tile, NB), lambda f, i, w: (f * tiles + i, 0))],
        ),
        out_shape=[jax.ShapeDtypeStruct((2 * fronts, per, RING * NB), BF16)] * 2
        + [jax.ShapeDtypeStruct((fronts * per, NB), F32)],
        compiler_params=pltpu.CompilerParams(vmem_limit_bytes=60 << 20),
        name="solve_both",
        cost_estimate=pl.CostEstimate(flops=12_000_000_000, bytes_accessed=18 << 20, transcendentals=0),
    )(where, rows, inv_hi, inv_lo, inv_hi, inv_lo)


STEPS = (
    (1, 0), (3, 0), (0, 1), (0, 3),
    (1, 1), (3, 3), (1, 3), (3, 1),
    (1, 2), (3, 2), (2, 0),
    (2, 1), (2, 3), (0, 2), (2, 2),
)


def scatter_kernel(sent_ref, arrived_ref, send, recv, local):
    s, r, c = lax.axis_index("sub"), lax.axis_index("row"), lax.axis_index("col")
    per_front = sent_ref.shape[0] // 2
    group = s * per_front + r
    x, z = 2 * s + r % 2, r // 2
    others, where_to = [], []
    for dx, dz in STEPS:
        tx, tz = (x + dx) % RING, (z + dz) % RING
        to = {"sub": tx // 2, "row": 2 * tz + tx % 2, "col": c}
        where_to.append(to)
        others.append(to["sub"] * per_front + to["row"])
    barrier = pltpu.get_barrier_semaphore()
    for to in where_to:
        pl.semaphore_signal(barrier, inc=1, device_id=to, device_id_type=MESH)
    pl.semaphore_wait(barrier, len(where_to))
    copies = [
        pltpu.make_async_remote_copy(
            src_ref=sent_ref.at[g],
            dst_ref=arrived_ref.at[group],
            send_sem=send.at[n],
            recv_sem=recv.at[n],
            device_id=to,
            device_id_type=MESH,
        )
        for n, (g, to) in enumerate(zip(others, where_to))
    ]
    for item in copies:
        item.start()
    keep = pltpu.make_async_copy(sent_ref.at[group], arrived_ref.at[group], local)
    keep.start()
    keep.wait()
    for item in copies:
        item.wait_recv()
    for item in copies:
        item.wait_send()


def scatter_rows(sent):
    others = sent.shape[0] - 1
    return pl.pallas_call(
        scatter_kernel,
        in_specs=[pl.BlockSpec(memory_space=pl.ANY)],
        out_specs=pl.BlockSpec(memory_space=pl.ANY),
        out_shape=jax.ShapeDtypeStruct(sent.shape, F32),
        scratch_shapes=[
            pltpu.SemaphoreType.DMA((others,)),
            pltpu.SemaphoreType.DMA((others,)),
            pltpu.SemaphoreType.DMA,
        ],
        compiler_params=pltpu.CompilerParams(
            collective_id=1, has_side_effects=True, vmem_limit_bytes=60 << 20
        ),
        name="scatter_rows",
    )(sent)


def gather_rows(source, index_ref, base, width):
    sub = lax.broadcasted_iota(jnp.int32, (8, width), 0)
    picked = None
    for r in range(8):
        row = jnp.broadcast_to(source[pl.ds(index_ref[base + r], 1), :], (8, width))
        picked = row if picked is None else jnp.where(sub == r, row, picked)
    return picked


def product_kernel(where_ref, order_ref, *refs):
    side, hi_ref, lo_ref, window_ref, out_ref, updated = refs
    split_z = side.shape[0] == RING

    total = None
    for at in range(2):
        c_hi, c_lo = split(jnp.concatenate([side[k, at] if split_z else side[at, k] for k in range(RING)], axis=1))
        t_hi, t_lo = hi_ref[at], lo_ref[at]
        part = dot3_nt(t_hi, t_lo, c_hi, c_lo)
        total = part if total is None else total + part
    updated[...] = window_ref[...] - total
    width = out_ref.shape[1]

    def group(s, carry):
        for q in range(2):
            base = pl.multiple_of(s * 16 + q * 8, 8)
            out_ref[pl.ds(base, 8), :] = gather_rows(updated, order_ref, base, width)
        return carry

    lax.fori_loop(0, out_ref.shape[0] // 16, group, 0)


def product(where, order, side, rows_hi, rows_lo, window, first, tile=512):
    _, rows, _ = rows_hi.shape
    outer, inner, tall, _ = side.shape
    tiles = tall // tile
    rows_spec = pl.BlockSpec(rows_hi.shape, lambda i, w, o: (0, 0, 0), pipeline_mode=pl.Buffered(1))
    return pl.pallas_call(
        product_kernel,
        grid_spec=pltpu.PrefetchScalarGridSpec(
            num_scalar_prefetch=2,
            grid=(tiles,),
            in_specs=[pl.BlockSpec((outer, inner, tile, NB), lambda i, w, o: (0, 0, i, 0))]
            + [rows_spec] * 2
            + [pl.BlockSpec((rows, tile), lambda i, w, o: (0, first * tiles + i))],
            out_specs=pl.BlockSpec((rows, tile), lambda i, w, o: (0, i)),
            scratch_shapes=[pltpu.VMEM((rows, tile), F32)],
        ),
        out_shape=jax.ShapeDtypeStruct((rows, tall), F32),
        compiler_params=pltpu.CompilerParams(vmem_limit_bytes=60 << 20),
        name="product",
        cost_estimate=pl.CostEstimate(flops=9_000_000_000, bytes_accessed=20 << 20, transcendentals=0),
    )(where, order, side, rows_hi, rows_lo, window)


def assemble_kernel(first_ref, second_ref, arrived_ref, *refs):
    out_ref = refs[-1]
    per, width = out_ref.shape

    def group(s, carry):
        for q in range(2):
            base = pl.multiple_of(s * 16 + q * 8, 8)
            out_ref[pl.ds(base, 8), :] = gather_rows(arrived_ref, first_ref, base, width) + gather_rows(
                arrived_ref, second_ref, base, width
            )
        return carry

    lax.fori_loop(0, per // 16, group, 0)


def assemble(place, arrived, parent, first, width, tile=512):
    total, cols = arrived.shape
    per = place.shape[0] // 2
    tiles = cols // tile
    extra = [] if parent is None else [parent]
    return pl.pallas_call(
        assemble_kernel,
        grid_spec=pltpu.PrefetchScalarGridSpec(
            num_scalar_prefetch=2,
            grid=(tiles,),
            in_specs=[pl.BlockSpec((total, tile), lambda i, p, q: (0, i))]
            + [pl.BlockSpec(memory_space=pl.ANY)] * len(extra),
            out_specs=pl.BlockSpec((per, tile), lambda i, p, q: (0, first * tiles + i)),
        ),
        out_shape=jax.ShapeDtypeStruct((per, width), F32),
        input_output_aliases={3: 0} if extra else {},
        compiler_params=pltpu.CompilerParams(vmem_limit_bytes=60 << 20),
        name="assemble",
        cost_estimate=pl.CostEstimate(flops=4_000_000, bytes_accessed=8 << 20, transcendentals=0),
    )(place[:per], place[per:], arrived, *extra)


def per_device(pivot_panel, border_panel, window, assembly_map):
    front = lax.axis_index("sub")
    row_index = lax.axis_index("row")
    col_index = lax.axis_index("col")
    fronts, n_row, n_col = lax.axis_size("sub"), lax.axis_size("row"), lax.axis_size("col")
    pivot_local, border_local, window_local = pivot_panel[0], border_panel[0], window[0]
    size = n_row * pivot_local.shape[0]
    rows_kept, width = window_local.shape
    groups = fronts * n_row
    per = rows_kept // fronts
    capacity = rows_kept // groups
    both = ("sub", "row")
    where = jnp.stack([front, row_index, col_index])

    def exchange(x):
        return lax.all_to_all(x, both, split_axis=0, concat_axis=0, tiled=True)

    targets, ordering = lax.sort((assembly_map[0], lax.iota(jnp.int32, rows_kept)), num_keys=1)
    slots = jnp.pad((targets % per).reshape(groups, 1, capacity), ((0, 0), (0, 7), (0, NB - capacity)))
    side_a, side_b, rows, rest, slots, inv_hi, inv_lo, pivot_factor = exchange_all(
        pivot_local, border_local, slots, rows_kept, size
    )
    rest, inv_hi, inv_lo = lax.optimization_barrier((rest, inv_hi, inv_lo))
    others = [rest]
    for d in (1, 2, 3):
        others.append(lax.ppermute(rest, "col", [(c, (c + 2 * d) % n_col) for c in range(n_col)]))

    owner = lax.iota(jnp.int32, rows_kept) // per
    _, place = lax.sort(
        (slots[:, 0, :capacity].reshape(-1) + owner * per, lax.iota(jnp.int32, rows_kept)), num_keys=1
    )

    rows_hi, rows_lo, border_kept = solve_both(where, rows, inv_hi, inv_lo)
    parent, arrived = None, []
    for first, side in enumerate((side_a, side_b)):
        sent = product(where, ordering, side, rows_hi, rows_lo, window_local, first)
        if first == 1:
            others, sent = lax.optimization_barrier((others, sent))
            border_rest = solve_rest(where, others, inv_hi, inv_lo)
            sent, border_rest = lax.optimization_barrier((sent, border_rest))
        move = exchange if first == 0 else scatter_rows
        arrived.append(move(sent.reshape(groups, capacity, -1)).reshape(rows_kept, -1))
    border_factor = jnp.concatenate([border_kept, border_rest], axis=0)
    for first in range(2):
        parent = assemble(place, arrived[first], parent, first, width)
    return (pivot_factor[None], border_factor[None], parent)


def solution(mesh):
    in_specs = (
        P("sub", "row", "col"),
        P("sub", "row", "col"),
        P("sub", "row", "col"),
        P("sub", "row"),
    )
    out_specs = (P("sub", "row", "col"), P("sub", "row", "col"), P(("sub", "row"), "col"))
    return jax.shard_map(
        per_device, mesh=mesh, in_specs=in_specs, out_specs=out_specs, check_vma=False
    )
```
